32 devices in a mesh: seq: 4 (over y, x), shard: 8 (over z, core).
Axes of the slice: x: 2, y: 2, z: 4, core: 2. Of those that a mesh axis runs over, the one named last changes fastest.
Arguments:
- tokens: bfloat16 [8, 1024, 2048], P('shard', 'seq'), may hold values from -6 to 6
- w_query: bfloat16 [2048, 2048], P('shard'), may hold values from -0.125 to 0.125
- w_key: bfloat16 [2048, 256], P('shard'), may hold values from -0.125 to 0.125
- w_value: bfloat16 [2048, 256], P('shard'), may hold values from -0.125 to 0.125
- w_out: bfloat16 [2048, 2048], P('shard'), may hold values from -1 to 1
- w_gate: bfloat16 [2048, 5632], P('shard'), may hold values from -0.125 to 0.125
- w_up: bfloat16 [2048, 5632], P('shard'), may hold values from -0.125 to 0.125
- w_down: bfloat16 [5632, 2048], P('shard'), may hold values from -0.078125 to 0.078125
- gain_attn: bfloat16 [2048], P('shard'), may hold values from 0.5 to 1.5
- gain_mlp: bfloat16 [2048], P('shard'), may hold values from 0.5 to 1.5
- cotangent: bfloat16 [8, 1024, 2048], P('shard', 'seq'), may hold values from -6 to 6
Outputs:
- output: bfloat16 [8, 1024, 2048], P('shard', 'seq')
- grad_tokens: float32 [8, 1024, 2048], P('shard', 'seq')
- grad_query: float32 [2048, 2048], P('shard')
- grad_key: float32 [2048, 256], P('shard')
- grad_value: float32 [2048, 256], P('shard')
- grad_out: float32 [2048, 2048], P('shard')
- grad_gate: float32 [2048, 5632], P('shard')
- grad_up: float32 [2048, 5632], P('shard')
- grad_down: float32 [5632, 2048], P('shard')
- grad_gain_attn: float32 [2048], P('shard')
- grad_gain_mlp: float32 [2048], P('shard')
The draws below stay inside these ranges and needn't reach their ends.
All inputs are finite; a program needn't handle non-finite values.
Results may differ from the reference program's by a relative error of at most 0.022.
Values may be sent and summed in bfloat16 or wider, within the bound.
No kernel may reach another device: no remote copies, remote signals or barrier semaphores. Data moves between devices by JAX's collectives and lax.ppermute only.
A program may use at most 384 MiB of HBM per device.

```python
import math
import jax
import jax.numpy as jnp
from jax import lax

D = 2048
FF = 5632
HEADS = 32
KV_HEADS = 4
HEAD_DIM = 64
SEQS = 8
SEQ_LEN = 1024
QWIDTH = 2048
KVWIDTH = 256
N_SEQ = 4


def steps_of(key, extent, shards, least, high):
    def one(axis_at, shards_of):
        heights = jax.random.uniform(jax.random.fold_in(jax.random.fold_in(key, 6), axis_at), (shards_of,), jnp.float32, least / len(shards), high / len(shards))
        return jnp.repeat(jnp.exp(heights), extent[axis_at] // shards_of).reshape((-1,) + (1,) * (len(extent) - axis_at - 1))

    loudness = one(*shards[0])
    for cut in shards[1:]:
        loudness = loudness * one(*cut)
    return loudness


def normal_values(rng, dims, width, reach, cuts=(), kind=jnp.bfloat16):
    loudness = steps_of(rng, dims, cuts, -0.22, 0.18) if cuts else 1.0
    entries = jax.random.normal(rng, dims, jnp.float32) * width * loudness
    return jnp.minimum(jnp.maximum(entries, -reach), reach).astype(kind)


def setup_inputs(seed: int = 0) -> dict:
    streams_of = jax.random.split(jax.random.key(seed), 12)
    tokens = normal_values(streams_of[0], (SEQS, SEQ_LEN, D), 1.0, 6.0, ((0, 8), (1, 4)))
    w_query = normal_values(streams_of[1], (D, QWIDTH), D ** -0.5, 0.125, ((0, 8),))
    w_key = normal_values(streams_of[2], (D, KVWIDTH), D ** -0.5, 0.125, ((0, 8),))
    w_value = normal_values(streams_of[3], (D, KVWIDTH), D ** -0.5, 0.125, ((0, 8),))
    w_out = normal_values(streams_of[4], (QWIDTH, D), (QWIDTH // 64) ** -0.5, 1.0, ((0, 8),))
    w_gate = normal_values(streams_of[5], (D, FF), D ** -0.5, 0.125, ((0, 8),))
    w_up = normal_values(streams_of[6], (D, FF), D ** -0.5, 0.125, ((0, 8),))
    w_down = normal_values(streams_of[7], (FF, D), FF ** -0.5, 0.078125, ((0, 8),))
    gain_attn = jnp.clip(1.0 + 0.1 * jax.random.normal(streams_of[8], (D,), jnp.float32), 0.5, 1.5).astype(jnp.bfloat16)
    gain_mlp = jnp.clip(1.0 + 0.1 * jax.random.normal(streams_of[9], (D,), jnp.float32), 0.5, 1.5).astype(jnp.bfloat16)
    cotangent = normal_values(streams_of[10], (SEQS, SEQ_LEN, D), 1.0, 6.0, ((0, 8), (1, 4)))
    return dict(tokens=tokens, w_query=w_query, w_key=w_key, w_value=w_value, w_out=w_out, w_gate=w_gate, w_up=w_up, w_down=w_down, gain_attn=gain_attn, gain_mlp=gain_mlp, cotangent=cotangent)


@jax.custom_vjp
def low(v):
    return lax.optimization_barrier(v.astype(jnp.bfloat16)).astype(jnp.float32)

@jax.custom_vjp
def low_back(v):
    return v

def low_keep(v):
    return (low(v), None)

def low_pass(kept, grad):
    return (grad,)

def back_keep(v):
    return (v, None)

def back_low(kept, grad):
    return (low(grad),)
low.defvjp(low_keep, low_pass)
low_back.defvjp(back_keep, back_low)
EPSILON = 1e-05
THETA = 10000.0

def round_both(values):
    return low_back(low(values))

def product(left, right):
    return jnp.dot(left, right, precision=lax.Precision.HIGHEST, preferred_element_type=jnp.float32)

def rms_norm(values):
    return values * lax.rsqrt(lax.optimization_barrier(jnp.mean(values * values, axis=-1, keepdims=True)) + EPSILON)

def rope_tables(length):
    half_dim = HEAD_DIM // 2
    frequency = jnp.exp(-math.log(THETA) * jnp.arange(half_dim).astype(jnp.float32) * 2.0 / HEAD_DIM)
    positions = jnp.arange(length).astype(jnp.float32)
    angles = positions[:, None] * frequency[None, :]
    return (jnp.cos(angles), jnp.sin(angles))

def rotate(head_array, cosine, sine_table):
    half_dim = head_array.shape[-1] // 2
    former = head_array[..., :half_dim]
    latter = head_array[..., half_dim:]
    cos_part = cosine[:, None, :]
    sin_part = sine_table[:, None, :]
    return jnp.concatenate([former * cos_part - latter * sin_part, latter * cos_part + former * sin_part], axis=-1)

def attend(queries, key_copies, value_copies):
    length = queries.shape[0]
    block_rows = min(512, length)
    spread = HEADS // key_copies.shape[1]
    key_all = jnp.repeat(key_copies, spread, axis=1)
    value_all = jnp.repeat(value_copies, spread, axis=1)
    score_scale = 1.0 / math.sqrt(HEAD_DIM)
    columns = jnp.arange(length).astype(jnp.int32)

    def one_block(start_row):
        query_rows = lax.dynamic_slice_in_dim(queries, start_row, block_rows, 0)
        scores = jnp.einsum('qhd,khd->hqk', query_rows, key_all, precision=lax.Precision.HIGHEST) * score_scale
        scores = low_back(scores)
        places = start_row + jnp.arange(block_rows).astype(jnp.int32)
        allowed = places[:, None] >= columns[None, :]
        scores = jnp.where(allowed[None], scores, -1e+30)
        highest = lax.optimization_barrier(jnp.max(scores, axis=-1, keepdims=True))
        exponent = jnp.exp(scores - highest)
        attn_probs = low(exponent / lax.optimization_barrier(jnp.sum(exponent, axis=-1, keepdims=True)))
        return jnp.einsum('hqk,khd->qhd', attn_probs, value_all, precision=lax.Precision.HIGHEST)
    starts = (jnp.arange(length // block_rows) * block_rows).astype(jnp.int32)
    pieces = lax.map(jax.checkpoint(one_block), starts)
    return pieces.reshape(length, HEADS, HEAD_DIM)

def layer(inputs, w_query, w_key, w_value, w_out, w_gate, w_up, w_down, gain_attn, gain_mlp):
    length = inputs.shape[0]
    cosine, sine_table = rope_tables(length)
    normed = low(rms_norm(inputs) * gain_attn)
    query_lin = low_back(product(normed, w_query)).reshape(length, HEADS, HEAD_DIM)
    key_lin = low_back(product(normed, w_key)).reshape(length, KV_HEADS, HEAD_DIM)
    queries = round_both(rotate(query_lin, cosine, sine_table))
    key_heads = round_both(rotate(key_lin, cosine, sine_table))
    value_heads = round_both(product(normed, w_value).reshape(length, KV_HEADS, HEAD_DIM))
    copies = max(1, N_SEQ // KV_HEADS)
    key_copies = low_back(jnp.repeat(key_heads, copies, axis=1))
    value_copies = low_back(jnp.repeat(value_heads, copies, axis=1))
    attended = round_both(attend(queries, key_copies, value_copies)).reshape(length, HEADS * HEAD_DIM)
    middle = inputs + low_back(product(attended, w_out))
    normed_mlp = low(rms_norm(middle) * gain_mlp)
    gate_lin = low_back(product(normed_mlp, w_gate))
    upward = low_back(product(normed_mlp, w_up))
    hidden = round_both(jax.nn.silu(gate_lin) * upward)
    return middle + low_back(product(hidden, w_down))

def reference(tokens, w_query, w_key, w_value, w_out, w_gate, w_up, w_down, gain_attn, gain_mlp, cotangent):
    params = tuple((entry.astype(jnp.float32) for entry in (w_query, w_key, w_value, w_out, w_gate, w_up, w_down, gain_attn, gain_mlp)))

    def one_sequence(running, couple):
        seq_inputs, seq_cotangent = couple
        result, pullback = jax.vjp(layer, seq_inputs.astype(jnp.float32), *params)
        gradients = pullback(seq_cotangent.astype(jnp.float32))
        running = tuple((summed + gradient for summed, gradient in zip(running, gradients[1:])))
        return (running, (result.astype(jnp.bfloat16), gradients[0]))
    initial = tuple((jnp.zeros(entry.shape, jnp.float32) for entry in params))
    totals, (output, grad_tokens) = lax.scan(one_sequence, initial, (tokens, cotangent))
    return (output, grad_tokens, totals[0], totals[1], totals[2], totals[3], totals[4], totals[5], totals[6], totals[7], totals[8])
```

```python
import functools
import math

import jax
import jax.numpy as jnp
from jax import lax
from jax.experimental import pallas as pl
from jax.experimental.pallas import tpu as pltpu
from jax.sharding import PartitionSpec as P

HEADS = 32
KV_HEADS = 4
HEAD_DIM = 64
PAIR = 2 * HEAD_DIM

EPSILON = 1e-05
THETA = 10000.0
MASKED = -1e30

f32 = jnp.float32
bf16 = jnp.bfloat16

NT = (((1,), (1,)), ((), ()))


def hop(value, bit):
    count = lax.axis_size("seq")
    return lax.ppermute(value, "seq", [(i, i ^ bit) for i in range(count)])


def gather_seq(block):
    count = lax.axis_size("seq")
    blocks = [block]
    if count >= 2:
        near = hop(block, 1)
        blocks.append(near)
    if count >= 4:
        other = hop(block, 2)
        half = block.shape[0] // 2
        far = jnp.concatenate([hop(near[:half], 2), hop(other[half:], 1)], axis=0)
        blocks += [other, far]
    bit = 4
    while bit < count:
        blocks += [hop(one, bit) for one in blocks]
        bit *= 2
    return blocks


def add_low(first, second):
    return (first.astype(f32) + second.astype(f32)).astype(bf16)


def scatter_seq(parts):
    count = lax.axis_size("seq")
    bit = count // 2
    while bit >= 4:
        there = [hop(parts[bit + r], bit) for r in range(bit)]
        parts = [add_low(parts[r], there[r]) for r in range(bit)]
        bit //= 2
    total = parts[0].astype(f32)
    if count >= 4:
        half = parts[3].shape[0] // 2
        upper = hop(parts[3][:half], 1)
        lower = hop(parts[3][half:], 2)
        kept_x = hop(parts[1][:half], 1)
        kept_y = hop(parts[2][half:], 2)
        sent_y = hop(add_low(parts[2][:half], upper), 2)
        sent_x = hop(add_low(parts[1][half:], lower), 1)
        total = total + jnp.concatenate([kept_x, sent_x], axis=0).astype(f32)
        total = total + jnp.concatenate([sent_y, kept_y], axis=0).astype(f32)
    elif count == 2:
        total = total + hop(parts[1], 1).astype(f32)
    return total


def in_order(stacked):
    count = stacked.shape[0]
    place = lax.axis_index("seq")
    bit = 1
    while bit < count:
        shaped = stacked.reshape((count // (2 * bit), 2, bit) + stacked.shape[1:])
        stacked = jnp.where((place & bit) != 0, shaped[:, ::-1], shaped).reshape(stacked.shape)
        bit *= 2
    return stacked


def rms_scale(values):
    return lax.rsqrt(jnp.mean(values * values, axis=-1, keepdims=True) + EPSILON)


def lane_in_first_half(shape):
    return lax.broadcasted_iota(jnp.int32, shape, 1) < HEAD_DIM


def swap_quarters(values):
    quarter = HEAD_DIM // 2
    lane = lax.broadcasted_iota(jnp.int32, values.shape, 1)
    return jnp.where(
        lane % HEAD_DIM < quarter,
        pltpu.roll(values, PAIR - quarter, 1),
        pltpu.roll(values, quarter, 1),
    )


def project_kernel(width_q, x_ref, gain_ref, w_ref, cos_ref, sin_ref, n_ref, q_ref, k_ref, v_ref):
    values = x_ref[0].astype(f32)
    scale = lax.rsqrt(jnp.mean(values * values, axis=-1, keepdims=True) + EPSILON)
    normed = (values * scale * gain_ref[...].astype(f32)).astype(bf16)
    n_ref[0] = normed
    lin = jnp.dot(normed, w_ref[...], preferred_element_type=f32)
    cosine, sine = cos_ref[0], sin_ref[0]
    for at in range(0, width_q, PAIR):
        part = lin[:, at : at + PAIR]
        turned = (part * cosine + swap_quarters(part) * sine).astype(bf16)
        q_ref[0, :, at : at + PAIR] = (turned.astype(f32) * HEAD_DIM**-0.5).astype(bf16)
    both = lin[:, width_q : width_q + PAIR]
    swapped = pltpu.roll(both, HEAD_DIM, 1)
    first = lane_in_first_half(both.shape)
    keys = jnp.where(first, both, swapped)
    k_ref[0] = (keys * cosine + swap_quarters(keys) * sine).astype(bf16)
    v_ref[0] = jnp.where(first, swapped, both).astype(bf16)


def project(x, gain, weights, cosine, sine, width_q):
    count, rows, width = x.shape
    row_block = lambda last: pl.BlockSpec((1, rows, last), lambda i: (i, 0, 0))
    whole = lambda shape: pl.BlockSpec(shape, lambda i: (0,) * len(shape))
    shape = lambda last: jax.ShapeDtypeStruct((count, rows, last), bf16)
    return pl.pallas_call(
        functools.partial(project_kernel, width_q),
        grid=(count,),
        in_specs=[
            row_block(width),
            whole((1, width)),
            whole(weights.shape),
            row_block(PAIR),
            row_block(PAIR),
        ],
        out_specs=[row_block(width), row_block(width_q), row_block(PAIR), row_block(PAIR)],
        out_shape=[shape(width), shape(width_q), shape(PAIR), shape(PAIR)],
        compiler_params=pltpu.CompilerParams(vmem_limit_bytes=40 * 2**20),
        cost_estimate=pl.CostEstimate(
            flops=2 * count * rows * width * (width_q + PAIR),
            bytes_accessed=6 * count * rows * width,
            transcendentals=0,
        ),
        name="project",
    )(x, gain, weights, cosine, sine)


def take_keys(count, rows, place, k_ref, v_ref, keys_of, values_of):
    for r in range(count):
        at = pl.multiple_of((place ^ r) * rows, rows)
        keys, values = k_ref[r], v_ref[r]
        first = lane_in_first_half(keys.shape)
        zero = jnp.zeros_like(keys)
        keys_of(0, at, jnp.where(first, keys, zero))
        keys_of(1, at, jnp.where(first, zero, keys))
        values_of(0, at, jnp.where(first, values, zero))
        values_of(1, at, jnp.where(first, zero, values))


def attend_kernel(
    count, rows, place_ref, q_ref, k_ref, v_ref, o_ref, l_ref, key_s, value_s, score_s
):
    block = pl.program_id(1)

    @pl.when((pl.program_id(0) == 0) & (block == 0))
    def _():
        def keys_of(h, at, value):
            key_s[h, pl.ds(at, rows), :] = value

        def values_of(h, at, value):
            value_s[h, :, pl.ds(at, rows)] = value.astype(f32).T.astype(bf16)

        take_keys(count, rows, place_ref[0], k_ref, v_ref, keys_of, values_of)

    key_at = lax.broadcasted_iota(jnp.int32, (rows, rows), 0)
    query_at = lax.broadcasted_iota(jnp.int32, (rows, rows), 1)
    allowed = key_at <= query_at

    for c in range(count):

        @pl.when(block == c)
        def _(c=c):
            queries = q_ref[0]
            total = None
            for h in range(2):
                highest = None
                for t in range(c + 1):
                    scores = lax.dot_general(
                        key_s[h, t * rows : (t + 1) * rows, :],
                        queries,
                        NT,
                        preferred_element_type=f32,
                    )
                    if t == c:
                        scores = jnp.where(allowed, scores, MASKED)
                    score_s[h, t * rows : (t + 1) * rows, :] = scores
                    top = jnp.max(scores, axis=0, keepdims=True)
                    highest = top if highest is None else jnp.maximum(highest, top)
                weight = None
                result = None
                for t in range(c + 1):
                    exponent = jnp.exp(score_s[h, t * rows : (t + 1) * rows, :] - highest)
                    one = jnp.sum(exponent, axis=0, keepdims=True)
                    weight = one if weight is None else weight + one
                    part = jnp.dot(
                        value_s[h, :, t * rows : (t + 1) * rows],
                        exponent.astype(bf16),
                        preferred_element_type=f32,
                    )
                    result = part if result is None else result + part
                l_ref[0, 0, h : h + 1, :] = highest + jnp.log(weight)
                result = result / weight
                total = result if total is None else total + result
            o_ref[0] = total.T.astype(bf16)


def attend(place, queries, keys, values):
    count, rows, width = queries.shape
    pairs = width // PAIR
    length = count * rows
    whole = pl.BlockSpec((count, rows, PAIR), lambda p, i, at: (0, 0, 0))
    mine = pl.BlockSpec((1, rows, PAIR), lambda p, i, at: (i ^ at[0], 0, p))
    return pl.pallas_call(
        functools.partial(attend_kernel, count, rows),
        grid_spec=pltpu.PrefetchScalarGridSpec(
            num_scalar_prefetch=1,
            grid=(pairs, count),
            in_specs=[mine, whole, whole],
            out_specs=[mine, pl.BlockSpec((1, 1, 8, rows), lambda p, i, at: (p, i, 0, 0))],
            scratch_shapes=[
                pltpu.VMEM((2, length, PAIR), bf16),
                pltpu.VMEM((2, PAIR, length), bf16),
                pltpu.VMEM((2, length, rows), f32),
            ],
        ),
        out_shape=[
            jax.ShapeDtypeStruct(queries.shape, bf16),
            jax.ShapeDtypeStruct((pairs, count, 8, rows), f32),
        ],
        compiler_params=pltpu.CompilerParams(vmem_limit_bytes=40 * 2**20),
        cost_estimate=pl.CostEstimate(
            flops=4 * pairs * length * length * PAIR,
            bytes_accessed=4 * length * width,
            transcendentals=pairs * length * length,
        ),
        name="attend",
    )(place, queries, keys, values)


def attend_back_kernel(
    count,
    rows,
    place_ref,
    q_ref,
    k_ref,
    v_ref,
    o_ref,
    d_ref,
    l_ref,
    cos_ref,
    sin_ref,
    dq_ref,
    dkv_ref,
    key_s,
    flat_s,
    value_s,
    dk_s,
    dv_s,
):
    pair, block = pl.program_id(0), pl.program_id(1)
    place = place_ref[0]

    @pl.when((pair == 0) & (block == 0))
    def _():
        def keys_of(h, at, value):
            key_s[h, pl.ds(at, rows), :] = value
            flat_s[h, :, pl.ds(at, rows)] = value.astype(f32).T.astype(bf16)

        def values_of(h, at, value):
            value_s[h, pl.ds(at, rows), :] = value

        take_keys(count, rows, place, k_ref, v_ref, keys_of, values_of)
        dk_s[...] = jnp.zeros_like(dk_s)
        dv_s[...] = jnp.zeros_like(dv_s)

    key_at = lax.broadcasted_iota(jnp.int32, (rows, rows), 0)
    query_at = lax.broadcasted_iota(jnp.int32, (rows, rows), 1)
    allowed = key_at <= query_at

    for c in range(count):

        @pl.when(block == c)
        def _(c=c):
            queries, back = q_ref[0], d_ref[0]
            first = lane_in_first_half(queries.shape)
            zero = jnp.zeros_like(queries)
            terms = (back.astype(f32) * o_ref[0].astype(f32)).T
            total = None
            for h in range(2):
                row_term = jnp.sum(
                    terms[h * HEAD_DIM : (h + 1) * HEAD_DIM, :], axis=0, keepdims=True
                )
                query_h = jnp.where(first, queries, zero) if h == 0 else jnp.where(first, zero, queries)
                back_h = jnp.where(first, back, zero) if h == 0 else jnp.where(first, zero, back)
                logsum = l_ref[0, 0, h : h + 1, :]
                for t in range(c + 1):
                    at = slice(t * rows, (t + 1) * rows)
                    scores = lax.dot_general(
                        key_s[h, at, :], queries, NT, preferred_element_type=f32
                    )
                    if t == c:
                        scores = jnp.where(allowed, scores, MASKED)
                    probs = jnp.exp(scores - logsum)
                    back_probs = lax.dot_general(
                        value_s[h, at, :], back, NT, preferred_element_type=f32
                    )
                    back_scores = (probs * (back_probs - row_term)).astype(bf16)
                    dv_s[at, :] += jnp.dot(
                        probs.astype(bf16), back_h, preferred_element_type=f32
                    )
                    dk_s[at, :] += jnp.dot(back_scores, query_h, preferred_element_type=f32)
                    part = jnp.dot(flat_s[h, :, at], back_scores, preferred_element_type=f32)
                    total = part if total is None else total + part
            turned = (total.T * HEAD_DIM**-0.5).astype(bf16).astype(f32)
            dq_ref[0] = (
                turned * cos_ref[block ^ place] - swap_quarters(turned) * sin_ref[block ^ place]
            ).astype(bf16)

    @pl.when((pair == pl.num_programs(0) - 1) & (block == pl.num_programs(1) - 1))
    def _():
        for r in range(count):
            at = pl.multiple_of((place ^ r) * rows, rows)
            keys = dk_s[pl.ds(at, rows), :]
            values = dv_s[pl.ds(at, rows), :]
            keys = (keys + pltpu.roll(keys, HEAD_DIM, 1)).astype(bf16).astype(f32)
            values = values + pltpu.roll(values, HEAD_DIM, 1)
            keys = keys * cos_ref[r] - swap_quarters(keys) * sin_ref[r]
            dkv_ref[r] = jnp.where(lane_in_first_half(keys.shape), keys, values).astype(bf16)


def attend_back(place, queries, keys, values, attended, back, logsum, cosine, sine):
    count, rows, width = queries.shape
    pairs = width // PAIR
    length = count * rows
    whole = pl.BlockSpec((count, rows, PAIR), lambda p, i, at: (0, 0, 0))
    mine = pl.BlockSpec((1, rows, PAIR), lambda p, i, at: (i ^ at[0], 0, p))
    return pl.pallas_call(
        functools.partial(attend_back_kernel, count, rows),
        grid_spec=pltpu.PrefetchScalarGridSpec(
            num_scalar_prefetch=1,
            grid=(pairs, count),
            in_specs=[
                mine,
                whole,
                whole,
                mine,
                mine,
                pl.BlockSpec((1, 1, 8, rows), lambda p, i, at: (p, i, 0, 0)),
                whole,
                whole,
            ],
            out_specs=[mine, whole],
            scratch_shapes=[
                pltpu.VMEM((2, length, PAIR), bf16),
                pltpu.VMEM((2, PAIR, length), bf16),
                pltpu.VMEM((2, length, PAIR), bf16),
                pltpu.VMEM((length, PAIR), f32),
                pltpu.VMEM((length, PAIR), f32),
            ],
        ),
        out_shape=[
            jax.ShapeDtypeStruct(queries.shape, bf16),
            jax.ShapeDtypeStruct((count, rows, PAIR), bf16),
        ],
        compiler_params=pltpu.CompilerParams(vmem_limit_bytes=40 * 2**20),
        cost_estimate=pl.CostEstimate(
            flops=10 * pairs * length * length * PAIR,
            bytes_accessed=8 * length * width,
            transcendentals=pairs * length * length,
        ),
        name="attend_back",
    )(place, queries, keys, values, attended, back, logsum, cosine, sine)


def on_device(
    tokens, w_query, w_key, w_value, w_out, w_gate, w_up, w_down, gain_attn, gain_mlp, cotangent
):
    count = lax.axis_size("seq")
    shards = lax.axis_size("shard")
    place = lax.axis_index("seq")
    mine = tokens[0]
    rows, width = mine.shape
    length = rows * count
    width_q = HEADS * HEAD_DIM // count
    local_kv = max(1, KV_HEADS // count)
    copies = count * local_kv // KV_HEADS
    width_kv = local_kv * HEAD_DIM
    assert width_kv == HEAD_DIM
    ff = w_gate.shape[1]
    piece = ff // (shards * count)
    width_f = shards * piece
    place_arg = place.reshape(1).astype(jnp.int32)

    def columns(weight, start, size):
        return lax.dynamic_slice_in_dim(weight, start, size, axis=1)

    def hidden_columns(weight):
        split = weight.reshape(weight.shape[0], shards, count, piece)
        return lax.dynamic_index_in_dim(split, place, axis=2, keepdims=False).reshape(
            weight.shape[0], width_f
        )

    def from_shards(block):
        return lax.all_gather(block, "shard", axis=0, tiled=True)

    kv_start = (place * local_kv // copies) * HEAD_DIM
    gains = lax.all_gather(jnp.stack([gain_attn, gain_mlp]), "shard", axis=1, tiled=True)
    gain_first, gain_second = gains[0:1], gains[1:2].astype(f32)
    w_qkv = from_shards(
        jnp.concatenate(
            [
                columns(w_query, place * width_q, width_q),
                columns(w_key, kv_start, width_kv),
                columns(w_value, kv_start, width_kv),
            ],
            axis=1,
        )
    )
    part_d = width // count
    w_o_columns = from_shards(columns(w_out, place * part_d, part_d))
    w_gu = from_shards(jnp.concatenate([hidden_columns(w_gate), hidden_columns(w_up)], axis=1))
    w_dn = from_shards(lax.dynamic_slice_in_dim(w_down, place * piece, piece, axis=0))

    inputs = jnp.stack(gather_seq(mine))
    back_mlp = jnp.concatenate(gather_seq(cotangent[0]))

    w_o = jnp.zeros((width_q, width), bf16)
    for r in range(count):
        rows_r = lax.dynamic_slice_in_dim(w_o_columns, (place ^ r) * width_q, width_q, axis=0)
        rows_r = hop(rows_r, r) if r else rows_r
        w_o = lax.dynamic_update_slice_in_dim(w_o, rows_r, (place ^ r) * part_d, axis=1)

    blocks_at = place ^ jnp.arange(count)
    positions = (blocks_at[:, None] * rows + jnp.arange(rows)[None, :]).astype(f32)
    half_dim = HEAD_DIM // 2
    lanes = jnp.arange(PAIR)
    frequency = jnp.exp(
        -math.log(THETA) * (lanes % half_dim).astype(f32) * 2.0 / HEAD_DIM
    )
    angles = positions[:, :, None] * frequency
    cosine = jnp.cos(angles)
    sine = jnp.sin(angles) * jnp.where(lanes % HEAD_DIM < half_dim, -1.0, 1.0)

    normed, queries, keys, values = project(inputs, gain_first, w_qkv, cosine, sine, width_q)
    attended, logsum = attend(place_arg, queries, keys, values)
    attended_rows = attended.reshape(length, width_q)

    def split(array):
        array = array.astype(bf16)
        return [array[r * rows : (r + 1) * rows] for r in range(count)]

    middle = mine.astype(f32) + scatter_seq(
        split(jnp.dot(attended_rows, w_o, preferred_element_type=f32))
    )
    scale_mid = rms_scale(middle)
    normed_mid = middle * scale_mid
    normed_mlp = jnp.concatenate(gather_seq((normed_mid * gain_second).astype(bf16)))

    gate_up = jnp.dot(normed_mlp, w_gu, preferred_element_type=f32)
    gate_lin, upward = gate_up[:, :width_f], gate_up[:, width_f:]
    sigmoid_gate = jax.nn.sigmoid(gate_lin)
    silu_gate = gate_lin * sigmoid_gate
    hidden = (silu_gate * upward).astype(bf16)
    back_hidden = (
        jnp.einsum("td,fd->tf", back_mlp, w_dn, preferred_element_type=f32).astype(bf16).astype(f32)
    )
    back_gate = back_hidden * upward * sigmoid_gate * (1.0 + gate_lin * (1.0 - sigmoid_gate))
    back_up = back_hidden * silu_gate
    back_gu = jnp.concatenate([back_gate.astype(bf16), back_up.astype(bf16)], axis=1)

    back_normed_mlp = scatter_seq(
        split(jnp.einsum("tf,df->td", back_gu, w_gu, preferred_element_type=f32))
    )
    output = middle + scatter_seq(split(jnp.dot(hidden, w_dn, preferred_element_type=f32)))
    output = output.astype(bf16)[None]

    def norm_back(values_in, scale, gain, back):
        branch = back * gain
        return scale * (
            branch - values_in * scale * scale * jnp.mean(branch * values_in, -1, keepdims=True)
        )

    out_grad = cotangent[0].astype(f32)
    gain_m_part = jnp.sum(back_normed_mlp * normed_mid, axis=0)
    back_middle = out_grad + norm_back(middle, scale_mid, gain_second, back_normed_mlp)
    back_branch = jnp.concatenate(gather_seq(back_middle.astype(bf16)))

    def to_owners(part):
        return lax.psum_scatter(part.astype(bf16), "shard", scatter_dimension=0, tiled=True)

    def token_sum(left, right):
        return jnp.einsum("tf,td->fd", left, right, preferred_element_type=f32)

    def whole_rows(owned):
        return in_order(jnp.stack(gather_seq(owned))).astype(f32)

    def whole_columns(owned):
        return jnp.swapaxes(whole_rows(owned), 0, 1)

    grad_down = whole_rows(to_owners(token_sum(hidden, back_mlp)))
    grad_down = grad_down.reshape(count * piece, width)
    own_gu = to_owners(token_sum(normed_mlp, back_gu))
    grad_gu = whole_rows(own_gu).reshape(count, -1, 2, shards, piece)
    grad_gu = grad_gu.transpose(2, 1, 3, 0, 4).reshape(2, -1, ff)

    back_attended = jnp.einsum("td,qd->tq", back_branch, w_o, preferred_element_type=f32)
    back_attended = back_attended.astype(bf16).reshape(count, rows, width_q)
    back_query, back_kv = attend_back(
        place_arg, queries, keys, values, attended, back_attended, logsum, cosine, sine
    )
    back_qkv = jnp.concatenate([back_query, back_kv], axis=2).reshape(length, -1)

    out_part = token_sum(attended_rows, back_branch).astype(bf16)
    out_columns = jnp.zeros((width_q * count, part_d), bf16)
    for r in range(count):
        part_r = lax.dynamic_slice_in_dim(out_part, (place ^ r) * part_d, part_d, axis=1)
        part_r = hop(part_r, r) if r else part_r
        out_columns = lax.dynamic_update_slice_in_dim(
            out_columns, part_r, (place ^ r) * width_q, axis=0
        )
    grad_out = whole_columns(to_owners(out_columns)).reshape(-1, width)

    own_qkv = to_owners(token_sum(normed.reshape(length, width), back_qkv))
    grad_qkv = whole_columns(own_qkv)
    grad_query = grad_qkv[:, :, :width_q].reshape(-1, HEADS * HEAD_DIM)

    def over_copies(part):
        part = part.reshape(-1, KV_HEADS // local_kv, copies, width_kv)
        return jnp.sum(part, axis=2).reshape(-1, KV_HEADS * HEAD_DIM)

    grad_key = over_copies(grad_qkv[:, :, width_q : width_q + width_kv])
    grad_value = over_copies(grad_qkv[:, :, width_q + width_kv :])

    back_normed = scatter_seq(
        split(jnp.einsum("tq,dq->td", back_qkv, w_qkv, preferred_element_type=f32))
    )
    mine_in = mine.astype(f32)
    scale_in = rms_scale(mine_in)
    gain_a_part = jnp.sum(back_normed * (mine_in * scale_in), axis=0)
    grad_tokens = back_middle + norm_back(
        mine_in, scale_in, gain_first.astype(f32), back_normed
    )
    gain_grads = lax.psum(jnp.stack([gain_a_part, gain_m_part]), ("seq", "shard"))
    owned = gain_attn.shape[0]
    gain_grads = lax.dynamic_slice_in_dim(
        gain_grads, lax.axis_index("shard") * owned, owned, axis=1
    )
    return (
        output,
        grad_tokens[None],
        grad_query,
        grad_key,
        grad_value,
        grad_out,
        grad_gu[0],
        grad_gu[1],
        grad_down,
        gain_grads[0],
        gain_grads[1],
    )


def solution(mesh):
    rows = P("shard", "seq", None)
    weight = P("shard", None)
    gain = P("shard")
    in_specs = (rows,) + (weight,) * 7 + (gain, gain, rows)
    out_specs = (rows, rows) + (weight,) * 7 + (gain, gain)
    return jax.shard_map(
        on_device, mesh=mesh, in_specs=in_specs, out_specs=out_specs, check_vma=False
    )
```

```python
import functools
import math

import jax
import jax.numpy as jnp
from jax import lax
from jax.experimental import pallas as pl
from jax.experimental.pallas import tpu as pltpu
from jax.sharding import PartitionSpec as P

HEADS = 32
KV_HEADS = 4
HEAD_DIM = 64
PAIR = 2 * HEAD_DIM

EPSILON = 1e-05
THETA = 10000.0
MASKED = -1e30

f32 = jnp.float32
bf16 = jnp.bfloat16

NT = (((1,), (1,)), ((), ()))


def hop(value, bit):
    count = lax.axis_size("seq")
    return lax.ppermute(value, "seq", [(i, i ^ bit) for i in range(count)])


def gather_seq(block):
    count = lax.axis_size("seq")
    blocks = [block]
    if count == 2:
        blocks.append(hop(block, 1))
    if count >= 4:
        half = block.shape[0] // 2
        upper, lower = block[:half], block[half:]
        near_upper, other_lower = hop(upper, 1), hop(lower, 2)
        near_lower, other_upper = hop(lower, 1), hop(upper, 2)
        far_upper, far_lower = hop(near_upper, 2), hop(other_lower, 1)
        blocks.append(jnp.concatenate([near_upper, near_lower], axis=0))
        blocks.append(jnp.concatenate([other_upper, other_lower], axis=0))
        blocks.append(jnp.concatenate([far_upper, far_lower], axis=0))
    bit = 4
    while bit < count:
        blocks += [hop(one, bit) for one in blocks]
        bit *= 2
    return blocks


def add_low(first, second):
    return (first.astype(f32) + second.astype(f32)).astype(bf16)


def tie(first, second):
    return lax.optimization_barrier((first, second))


def scatter_seq(parts, filler=None):
    count = lax.axis_size("seq")
    bit = count // 2
    while bit >= 4:
        there = [hop(parts[bit + r], bit) for r in range(bit)]
        parts = [add_low(parts[r], there[r]) for r in range(bit)]
        bit //= 2
    total = parts[0].astype(f32)
    if count >= 4:
        half = parts[3].shape[0] // 2
        upper = hop(parts[3][:half], 1)
        lower = hop(parts[3][half:], 2)
        kept_x = hop(parts[1][:half], 1)
        kept_y = hop(parts[2][half:], 2)
        if filler is not None:
            (upper, lower), filler = tie((upper, lower), filler)
        sent_y = hop(add_low(parts[2][:half], upper), 2)
        sent_x = hop(add_low(parts[1][half:], lower), 1)
        total = total + jnp.concatenate([kept_x, sent_x], axis=0).astype(f32)
        total = total + jnp.concatenate([sent_y, kept_y], axis=0).astype(f32)
    elif count == 2:
        total = total + hop(parts[1], 1).astype(f32)
    return total if filler is None else (total, filler)


def rms_scale(values):
    return lax.rsqrt(jnp.mean(values * values, axis=-1, keepdims=True) + EPSILON)


def lane_in_first_half(shape):
    return lax.broadcasted_iota(jnp.int32, shape, 1) < HEAD_DIM


def swap_quarters(values):
    quarter = HEAD_DIM // 2
    lane = lax.broadcasted_iota(jnp.int32, values.shape, 1)
    return jnp.where(
        lane % HEAD_DIM < quarter,
        pltpu.roll(values, PAIR - quarter, 1),
        pltpu.roll(values, quarter, 1),
    )


def project_kernel(width_q, x_ref, gain_ref, w_ref, cos_ref, sin_ref, n_ref, q_ref, k_ref, v_ref):
    values = x_ref[0].astype(f32)
    scale = lax.rsqrt(jnp.mean(values * values, axis=-1, keepdims=True) + EPSILON)
    normed = (values * scale * gain_ref[...].astype(f32)).astype(bf16)
    n_ref[0] = normed
    lin = jnp.dot(normed, w_ref[...], preferred_element_type=f32)
    cosine, sine = cos_ref[0], sin_ref[0]
    for at in range(0, width_q, PAIR):
        part = lin[:, at : at + PAIR]
        turned = (part * cosine + swap_quarters(part) * sine).astype(bf16)
        q_ref[0, :, at : at + PAIR] = (turned.astype(f32) * HEAD_DIM**-0.5).astype(bf16)
    both = lin[:, width_q : width_q + PAIR]
    swapped = pltpu.roll(both, HEAD_DIM, 1)
    first = lane_in_first_half(both.shape)
    keys = jnp.where(first, both, swapped)
    k_ref[0] = (keys * cosine + swap_quarters(keys) * sine).astype(bf16)
    v_ref[0] = jnp.where(first, swapped, both).astype(bf16)


def project(x, gain, weights, cosine, sine, width_q):
    count, rows, width = x.shape
    row_block = lambda last: pl.BlockSpec((1, rows, last), lambda i: (i, 0, 0))
    whole = lambda shape: pl.BlockSpec(shape, lambda i: (0,) * len(shape))
    shape = lambda last: jax.ShapeDtypeStruct((count, rows, last), bf16)
    return pl.pallas_call(
        functools.partial(project_kernel, width_q),
        grid=(count,),
        in_specs=[
            row_block(width),
            whole((1, width)),
            whole(weights.shape),
            row_block(PAIR),
            row_block(PAIR),
        ],
        out_specs=[row_block(width), row_block(width_q), row_block(PAIR), row_block(PAIR)],
        out_shape=[shape(width), shape(width_q), shape(PAIR), shape(PAIR)],
        compiler_params=pltpu.CompilerParams(vmem_limit_bytes=40 * 2**20),
        cost_estimate=pl.CostEstimate(
            flops=2 * count * rows * width * (width_q + PAIR),
            bytes_accessed=6 * count * rows * width,
            transcendentals=0,
        ),
        name="project",
    )(x, gain, weights, cosine, sine)


def take_keys(count, rows, place, k_ref, v_ref, keys_of, values_of):
    for r in range(count):
        at = pl.multiple_of((place ^ r) * rows, rows)
        keys, values = k_ref[r], v_ref[r]
        first = lane_in_first_half(keys.shape)
        zero = jnp.zeros_like(keys)
        keys_of(0, at, jnp.where(first, keys, zero))
        keys_of(1, at, jnp.where(first, zero, keys))
        values_of(0, at, jnp.where(first, values, zero))
        values_of(1, at, jnp.where(first, zero, values))


def attend_kernel(
    count, rows, place_ref, q_ref, k_ref, v_ref, o_ref, l_ref, key_s, value_s, score_s
):
    block = pl.program_id(1)

    @pl.when((pl.program_id(0) == 0) & (block == 0))
    def _():
        def keys_of(h, at, value):
            key_s[h, pl.ds(at, rows), :] = value

        def values_of(h, at, value):
            value_s[h, :, pl.ds(at, rows)] = value.astype(f32).T.astype(bf16)

        take_keys(count, rows, place_ref[0], k_ref, v_ref, keys_of, values_of)

    key_at = lax.broadcasted_iota(jnp.int32, (rows, rows), 0)
    query_at = lax.broadcasted_iota(jnp.int32, (rows, rows), 1)
    allowed = key_at <= query_at

    for c in range(count):

        @pl.when(block == c)
        def _(c=c):
            queries = q_ref[0]
            total = None
            for h in range(2):
                highest = None
                for t in range(c + 1):
                    scores = lax.dot_general(
                        key_s[h, t * rows : (t + 1) * rows, :],
                        queries,
                        NT,
                        preferred_element_type=f32,
                    )
                    if t == c:
                        scores = jnp.where(allowed, scores, MASKED)
                    score_s[h, t * rows : (t + 1) * rows, :] = scores
                    top = jnp.max(scores, axis=0, keepdims=True)
                    highest = top if highest is None else jnp.maximum(highest, top)
                weight = None
                result = None
                for t in range(c + 1):
                    exponent = jnp.exp(score_s[h, t * rows : (t + 1) * rows, :] - highest)
                    one = jnp.sum(exponent, axis=0, keepdims=True)
                    weight = one if weight is None else weight + one
                    part = jnp.dot(
                        value_s[h, :, t * rows : (t + 1) * rows],
                        exponent.astype(bf16),
                        preferred_element_type=f32,
                    )
                    result = part if result is None else result + part
                l_ref[0, 0, h : h + 1, :] = highest + jnp.log(weight)
                result = result / weight
                total = result if total is None else total + result
            o_ref[0] = total.T.astype(bf16)


def attend(place, queries, keys, values):
    count, rows, width = queries.shape
    pairs = width // PAIR
    length = count * rows
    whole = pl.BlockSpec((count, rows, PAIR), lambda p, i, at: (0, 0, 0))
    mine = pl.BlockSpec((1, rows, PAIR), lambda p, i, at: (i ^ at[0], 0, p))
    return pl.pallas_call(
        functools.partial(attend_kernel, count, rows),
        grid_spec=pltpu.PrefetchScalarGridSpec(
            num_scalar_prefetch=1,
            grid=(pairs, count),
            in_specs=[mine, whole, whole],
            out_specs=[mine, pl.BlockSpec((1, 1, 8, rows), lambda p, i, at: (p, i, 0, 0))],
            scratch_shapes=[
                pltpu.VMEM((2, length, PAIR), bf16),
                pltpu.VMEM((2, PAIR, length), bf16),
                pltpu.VMEM((2, length, rows), f32),
            ],
        ),
        out_shape=[
            jax.ShapeDtypeStruct(queries.shape, bf16),
            jax.ShapeDtypeStruct((pairs, count, 8, rows), f32),
        ],
        compiler_params=pltpu.CompilerParams(vmem_limit_bytes=40 * 2**20),
        cost_estimate=pl.CostEstimate(
            flops=4 * pairs * length * length * PAIR,
            bytes_accessed=4 * length * width,
            transcendentals=pairs * length * length,
        ),
        name="attend",
    )(place, queries, keys, values)


def attend_back_kernel(
    count,
    rows,
    place_ref,
    q_ref,
    k_ref,
    v_ref,
    o_ref,
    d_ref,
    l_ref,
    cos_ref,
    sin_ref,
    dq_ref,
    dkv_ref,
    key_s,
    flat_s,
    value_s,
    dk_s,
    dv_s,
):
    pair, block = pl.program_id(0), pl.program_id(1)
    place = place_ref[0]

    @pl.when((pair == 0) & (block == 0))
    def _():
        def keys_of(h, at, value):
            key_s[h, pl.ds(at, rows), :] = value
            flat_s[h, :, pl.ds(at, rows)] = value.astype(f32).T.astype(bf16)

        def values_of(h, at, value):
            value_s[h, pl.ds(at, rows), :] = value

        take_keys(count, rows, place, k_ref, v_ref, keys_of, values_of)
        dk_s[...] = jnp.zeros_like(dk_s)
        dv_s[...] = jnp.zeros_like(dv_s)

    key_at = lax.broadcasted_iota(jnp.int32, (rows, rows), 0)
    query_at = lax.broadcasted_iota(jnp.int32, (rows, rows), 1)
    allowed = key_at <= query_at

    for c in range(count):

        @pl.when(block == c)
        def _(c=c):
            queries, back = q_ref[0], d_ref[0]
            first = lane_in_first_half(queries.shape)
            zero = jnp.zeros_like(queries)
            terms = (back.astype(f32) * o_ref[0].astype(f32)).T
            total = None
            for h in range(2):
                row_term = jnp.sum(
                    terms[h * HEAD_DIM : (h + 1) * HEAD_DIM, :], axis=0, keepdims=True
                )
                query_h = jnp.where(first, queries, zero) if h == 0 else jnp.where(first, zero, queries)
                back_h = jnp.where(first, back, zero) if h == 0 else jnp.where(first, zero, back)
                logsum = l_ref[0, 0, h : h + 1, :]
                for t in range(c + 1):
                    at = slice(t * rows, (t + 1) * rows)
                    scores = lax.dot_general(
                        key_s[h, at, :], queries, NT, preferred_element_type=f32
                    )
                    if t == c:
                        scores = jnp.where(allowed, scores, MASKED)
                    probs = jnp.exp(scores - logsum)
                    back_probs = lax.dot_general(
                        value_s[h, at, :], back, NT, preferred_element_type=f32
                    )
                    back_scores = (probs * (back_probs - row_term)).astype(bf16)
                    dv_s[at, :] += jnp.dot(
                        probs.astype(bf16), back_h, preferred_element_type=f32
                    )
                    dk_s[at, :] += jnp.dot(back_scores, query_h, preferred_element_type=f32)
                    part = jnp.dot(flat_s[h, :, at], back_scores, preferred_element_type=f32)
                    total = part if total is None else total + part
            turned = (total.T * HEAD_DIM**-0.5).astype(bf16).astype(f32)
            dq_ref[0] = (
                turned * cos_ref[block ^ place] - swap_quarters(turned) * sin_ref[block ^ place]
            ).astype(bf16)

    @pl.when((pair == pl.num_programs(0) - 1) & (block == pl.num_programs(1) - 1))
    def _():
        for r in range(count):
            at = pl.multiple_of((place ^ r) * rows, rows)
            keys = dk_s[pl.ds(at, rows), :]
            values = dv_s[pl.ds(at, rows), :]
            keys = (keys + pltpu.roll(keys, HEAD_DIM, 1)).astype(bf16).astype(f32)
            values = values + pltpu.roll(values, HEAD_DIM, 1)
            keys = keys * cos_ref[r] - swap_quarters(keys) * sin_ref[r]
            dkv_ref[r] = jnp.where(lane_in_first_half(keys.shape), keys, values).astype(bf16)


def attend_back(place, queries, keys, values, attended, back, logsum, cosine, sine):
    count, rows, width = queries.shape
    pairs = width // PAIR
    length = count * rows
    whole = pl.BlockSpec((count, rows, PAIR), lambda p, i, at: (0, 0, 0))
    mine = pl.BlockSpec((1, rows, PAIR), lambda p, i, at: (i ^ at[0], 0, p))
    return pl.pallas_call(
        functools.partial(attend_back_kernel, count, rows),
        grid_spec=pltpu.PrefetchScalarGridSpec(
            num_scalar_prefetch=1,
            grid=(pairs, count),
            in_specs=[
                mine,
                whole,
                whole,
                mine,
                mine,
                pl.BlockSpec((1, 1, 8, rows), lambda p, i, at: (p, i, 0, 0)),
                whole,
                whole,
            ],
            out_specs=[mine, whole],
            scratch_shapes=[
                pltpu.VMEM((2, length, PAIR), bf16),
                pltpu.VMEM((2, PAIR, length), bf16),
                pltpu.VMEM((2, length, PAIR), bf16),
                pltpu.VMEM((length, PAIR), f32),
                pltpu.VMEM((length, PAIR), f32),
            ],
        ),
        out_shape=[
            jax.ShapeDtypeStruct(queries.shape, bf16),
            jax.ShapeDtypeStruct((count, rows, PAIR), bf16),
        ],
        compiler_params=pltpu.CompilerParams(vmem_limit_bytes=40 * 2**20),
        cost_estimate=pl.CostEstimate(
            flops=10 * pairs * length * length * PAIR,
            bytes_accessed=8 * length * width,
            transcendentals=pairs * length * length,
        ),
        name="attend_back",
    )(place, queries, keys, values, attended, back, logsum, cosine, sine)


def sort_blocks(place, blocks):
    bit = 1
    while bit < len(blocks):
        flip = (place & bit) != 0
        blocks = [
            jnp.where(flip, blocks[r ^ bit], blocks[r]) for r in range(len(blocks))
        ]
        bit *= 2
    return blocks


def take_columns_kernel(shards, count, piece, place_ref, gate_ref, up_ref, out_ref):
    width = shards * piece
    for c in range(count):

        @pl.when(place_ref[0] == c)
        def _(c=c):
            for at, ref in ((0, gate_ref), (width, up_ref)):
                pieces = []
                for s in range(shards):
                    start = (s * count + c) * piece
                    pieces.append(ref[:, start : start + piece].astype(f32))
                out_ref[:, at : at + width] = jnp.concatenate(pieces, axis=1).astype(bf16)


def take_columns(place, w_gate, w_up, shards, count):
    rows, ff = w_gate.shape
    piece = ff // (shards * count)
    step = min(rows, 128)
    block = lambda last: pl.BlockSpec((step, last), lambda i, at: (i, 0))
    return pl.pallas_call(
        functools.partial(take_columns_kernel, shards, count, piece),
        grid_spec=pltpu.PrefetchScalarGridSpec(
            num_scalar_prefetch=1,
            grid=(rows // step,),
            in_specs=[block(ff), block(ff)],
            out_specs=block(2 * shards * piece),
        ),
        out_shape=jax.ShapeDtypeStruct((rows, 2 * shards * piece), bf16),
        compiler_params=pltpu.CompilerParams(vmem_limit_bytes=40 * 2**20),
        cost_estimate=pl.CostEstimate(
            flops=0, bytes_accessed=6 * rows * ff, transcendentals=0
        ),
        name="take_columns",
    )(place, w_gate, w_up)


def put_columns_kernel(shards, count, piece, place_ref, *refs):
    block_refs = refs[:count]
    gate_w, up_w, gain_ref, gate_ref, up_ref, gain_out = refs[count:]
    width = shards * piece
    blocks = [ref[...].astype(f32) for ref in block_refs]
    blocks = sort_blocks(place_ref[0], blocks)
    total = None
    for at, weight, out in ((0, gate_w, gate_ref), (width, up_w, up_ref)):
        for s in range(shards):
            pieces = [one[:, at + s * piece : at + (s + 1) * piece] for one in blocks]
            joined = jnp.concatenate(pieces, axis=1)
            here = slice(s * count * piece, (s + 1) * count * piece)
            out[:, here] = joined
            term = jnp.sum(joined * weight[:, here].astype(f32), axis=1, keepdims=True)
            total = term if total is None else total + term
    gain_out[...] = total / gain_ref[...].astype(f32)


def put_columns(place, blocks, w_gate, w_up, gain, shards):
    count = len(blocks)
    rows, ff = w_gate.shape
    piece = ff // (shards * count)
    step = min(rows, 64)
    block = lambda last: pl.BlockSpec((step, last), lambda i, at: (i, 0))
    return pl.pallas_call(
        functools.partial(put_columns_kernel, shards, count, piece),
        grid_spec=pltpu.PrefetchScalarGridSpec(
            num_scalar_prefetch=1,
            grid=(rows // step,),
            in_specs=[block(blocks[0].shape[1])] * count + [block(ff), block(ff), block(1)],
            out_specs=[block(ff), block(ff), block(1)],
        ),
        out_shape=[
            jax.ShapeDtypeStruct((rows, ff), f32),
            jax.ShapeDtypeStruct((rows, ff), f32),
            jax.ShapeDtypeStruct((rows, 1), f32),
        ],
        compiler_params=pltpu.CompilerParams(vmem_limit_bytes=40 * 2**20),
        cost_estimate=pl.CostEstimate(
            flops=0, bytes_accessed=16 * rows * ff, transcendentals=0
        ),
        name="put_columns",
    )(place, *blocks, w_gate, w_up, gain)


def put_attention_kernel(count, copies, width_q, place_ref, *refs):
    block_refs = refs[:count]
    q_w, k_w, v_w, gain_ref, q_ref, k_ref, v_ref, o_ref, gain_out = refs[count:]
    blocks = [ref[...].astype(f32) for ref in block_refs]
    blocks = sort_blocks(place_ref[0], blocks)
    width_o = o_ref.shape[1] // count
    for a in range(count):
        q_ref[:, a * width_q : (a + 1) * width_q] = blocks[a][:, :width_q]
        o_ref[:, a * width_o : (a + 1) * width_o] = blocks[a][:, width_q + PAIR :]
    for part, out in ((0, k_ref), (HEAD_DIM, v_ref)):
        heads = []
        for h in range(count // copies):
            one = None
            for c in range(copies):
                at = width_q + part
                term = blocks[h * copies + c][:, at : at + HEAD_DIM]
                one = term if one is None else one + term
            heads.append(one)
        out[...] = jnp.concatenate(heads, axis=1)
    total = None
    for weight, out in ((q_w, q_ref), (k_w, k_ref), (v_w, v_ref)):
        term = jnp.sum(out[...] * weight[...].astype(f32), axis=1, keepdims=True)
        total = term if total is None else total + term
    gain_out[...] = total / gain_ref[...].astype(f32)


def put_attention(place, blocks, w_query, w_key, w_value, gain, width, copies):
    count = len(blocks)
    rows, wide_q = w_query.shape
    wide_k = w_key.shape[1]
    step = min(rows, 64)
    block = lambda last: pl.BlockSpec((step, last), lambda i, at: (i, 0))
    return pl.pallas_call(
        functools.partial(put_attention_kernel, count, copies, wide_q // count),
        grid_spec=pltpu.PrefetchScalarGridSpec(
            num_scalar_prefetch=1,
            grid=(rows // step,),
            in_specs=[block(blocks[0].shape[1])] * count
            + [block(wide_q), block(wide_k), block(wide_k), block(1)],
            out_specs=[block(wide_q), block(wide_k), block(wide_k), block(width), block(1)],
        ),
        out_shape=[
            jax.ShapeDtypeStruct((rows, last), f32) for last in (wide_q, wide_k, wide_k, width, 1)
        ],
        compiler_params=pltpu.CompilerParams(vmem_limit_bytes=40 * 2**20),
        cost_estimate=pl.CostEstimate(
            flops=0, bytes_accessed=16 * rows * wide_q, transcendentals=0
        ),
        name="put_attention",
    )(place, *blocks, w_query, w_key, w_value, gain)


def on_device(
    tokens, w_query, w_key, w_value, w_out, w_gate, w_up, w_down, gain_attn, gain_mlp, cotangent
):
    count = lax.axis_size("seq")
    shards = lax.axis_size("shard")
    place = lax.axis_index("seq")
    mine = tokens[0]
    rows, width = mine.shape
    length = rows * count
    width_q = HEADS * HEAD_DIM // count
    local_kv = max(1, KV_HEADS // count)
    copies = count * local_kv // KV_HEADS
    width_kv = local_kv * HEAD_DIM
    assert width_kv == HEAD_DIM
    ff = w_gate.shape[1]
    piece = ff // (shards * count)
    width_f = shards * piece
    place_arg = place.reshape(1).astype(jnp.int32)

    def columns(weight, start, size):
        return lax.dynamic_slice_in_dim(weight, start, size, axis=1)

    def from_shards(block):
        return lax.all_gather(block, "shard", axis=0, tiled=True)

    kv_start = (place * local_kv // copies) * HEAD_DIM
    part_d = width // count
    width_qkv = width_q + PAIR
    gains = lax.all_gather(jnp.stack([gain_attn, gain_mlp]), "shard", axis=1, tiled=True)
    gain_first, gain_second = gains[0:1], gains[1:2].astype(f32)
    w_attn = from_shards(
        jnp.concatenate(
            [
                columns(w_query, place * width_q, width_q),
                columns(w_key, kv_start, width_kv),
                columns(w_value, kv_start, width_kv),
                columns(w_out, place * part_d, part_d),
            ],
            axis=1,
        )
    )
    w_qkv, w_o_columns = w_attn[:, :width_qkv], w_attn[:, width_qkv:]
    w_gu = from_shards(take_columns(place_arg, w_gate, w_up, shards, count))
    w_dn = from_shards(lax.dynamic_slice_in_dim(w_down, place * piece, piece, axis=0))

    inputs = jnp.stack(gather_seq(mine))

    w_o = jnp.zeros((width_q, width), bf16)
    for r in range(count):
        rows_r = lax.dynamic_slice_in_dim(w_o_columns, (place ^ r) * width_q, width_q, axis=0)
        rows_r = hop(rows_r, r) if r else rows_r
        w_o = lax.dynamic_update_slice_in_dim(w_o, rows_r, (place ^ r) * part_d, axis=1)

    blocks_at = place ^ jnp.arange(count)
    positions = (blocks_at[:, None] * rows + jnp.arange(rows)[None, :]).astype(f32)
    half_dim = HEAD_DIM // 2
    lanes = jnp.arange(PAIR)
    frequency = jnp.exp(-math.log(THETA) * (lanes % half_dim).astype(f32) * 2.0 / HEAD_DIM)
    angles = positions[:, :, None] * frequency
    cosine = jnp.cos(angles)
    sine = jnp.sin(angles) * jnp.where(lanes % HEAD_DIM < half_dim, -1.0, 1.0)

    normed, queries, keys, values = project(inputs, gain_first, w_qkv, cosine, sine, width_q)
    attended, logsum = attend(place_arg, queries, keys, values)
    attended_rows = attended.reshape(length, width_q)

    def split(array):
        array = array.astype(bf16)
        return [array[r * rows : (r + 1) * rows] for r in range(count)]

    def token_sum(left, right):
        return jnp.einsum("tf,td->fd", left, right, preferred_element_type=f32).astype(bf16)

    def to_owners(part):
        return lax.psum_scatter(part, "shard", scatter_dimension=0, tiled=True)

    def norm_back(values_in, scale, gain, back):
        branch = back * gain
        return scale * (
            branch - values_in * scale * scale * jnp.mean(branch * values_in, -1, keepdims=True)
        )

    middle = mine.astype(f32) + scatter_seq(
        split(jnp.dot(attended_rows, w_o, preferred_element_type=f32))
    )
    scale_mid = rms_scale(middle)
    normed_blocks = gather_seq((middle * scale_mid * gain_second).astype(bf16))
    normed_blocks, cot = tie(normed_blocks, cotangent[0])
    normed_mlp = jnp.concatenate(normed_blocks)
    back_mlp = jnp.concatenate(gather_seq(cot))

    gate_up = jnp.dot(normed_mlp, w_gu, preferred_element_type=f32)
    gate_lin, upward = gate_up[:, :width_f], gate_up[:, width_f:]
    sigmoid_gate = jax.nn.sigmoid(gate_lin)
    silu_gate = gate_lin * sigmoid_gate
    hidden = (silu_gate * upward).astype(bf16)
    down_part = token_sum(hidden, back_mlp)
    own_down = to_owners(down_part)

    w_dn, down_part = tie(w_dn, down_part)
    back_hidden = (
        jnp.einsum("td,fd->tf", back_mlp, w_dn, preferred_element_type=f32).astype(bf16).astype(f32)
    )
    back_gate = back_hidden * upward * sigmoid_gate * (1.0 + gate_lin * (1.0 - sigmoid_gate))
    back_up = back_hidden * silu_gate
    back_gu = jnp.concatenate([back_gate.astype(bf16), back_up.astype(bf16)], axis=1)

    parts = split(jnp.einsum("tf,df->td", back_gu, w_gu, preferred_element_type=f32))
    back_normed_mlp, gu_part = scatter_seq(parts, token_sum(normed_mlp, back_gu))
    own_gu = to_owners(gu_part)

    back_middle = cot.astype(f32) + norm_back(middle, scale_mid, gain_second, back_normed_mlp)
    back_blocks = gather_seq(back_middle.astype(bf16))
    out_parts = split(jnp.dot(hidden, w_dn, preferred_element_type=f32))
    back_blocks, (out_parts, own_down) = tie(back_blocks, (out_parts, own_down))
    back_branch = jnp.concatenate(back_blocks)
    output = (middle + scatter_seq(out_parts)).astype(bf16)[None]

    back_attended = jnp.einsum("td,qd->tq", back_branch, w_o, preferred_element_type=f32)
    back_attended = back_attended.astype(bf16).reshape(count, rows, width_q)
    out_part = token_sum(attended_rows, back_branch)
    back_attended, out_part = tie(back_attended, out_part)
    back_query, back_kv = attend_back(
        place_arg, queries, keys, values, attended, back_attended, logsum, cosine, sine
    )
    back_qkv = jnp.concatenate([back_query, back_kv], axis=2).reshape(length, -1)

    attn_part = jnp.zeros((width, width_qkv + part_d), bf16)
    for r in range(count):
        part_r = lax.dynamic_slice_in_dim(out_part, (place ^ r) * part_d, part_d, axis=1)
        part_r = hop(part_r, r) if r else part_r
        attn_part = lax.dynamic_update_slice(attn_part, part_r, ((place ^ r) * width_q, width_qkv))
    qkv_part = token_sum(normed.reshape(length, width), back_qkv)
    own_attn = to_owners(lax.dynamic_update_slice(attn_part, qkv_part, (0, 0)))

    parts = split(jnp.einsum("tq,dq->td", back_qkv, w_qkv, preferred_element_type=f32))
    back_normed = scatter_seq(parts)
    mine_in = mine.astype(f32)
    grad_tokens = back_middle + norm_back(
        mine_in, rms_scale(mine_in), gain_first.astype(f32), back_normed
    )

    grad_down = jnp.zeros((count * piece, width), f32)
    for r, block in enumerate(gather_seq(own_down)):
        grad_down = lax.dynamic_update_slice_in_dim(
            grad_down, block.astype(f32), (place ^ r) * piece, axis=0
        )
    grad_gate, grad_up, grad_gain_mlp = put_columns(
        place_arg, gather_seq(own_gu), w_gate, w_up, gain_mlp.reshape(-1, 1), shards
    )
    grad_query, grad_key, grad_value, grad_out, grad_gain_attn = put_attention(
        place_arg,
        gather_seq(own_attn),
        w_query,
        w_key,
        w_value,
        gain_attn.reshape(-1, 1),
        width,
        copies,
    )
    return (
        output,
        grad_tokens[None],
        grad_query,
        grad_key,
        grad_value,
        grad_out,
        grad_gate,
        grad_up,
        grad_down,
        grad_gain_attn.reshape(-1),
        grad_gain_mlp.reshape(-1),
    )


def solution(mesh):
    rows = P("shard", "seq", None)
    weight = P("shard", None)
    gain = P("shard")
    in_specs = (rows,) + (weight,) * 7 + (gain, gain, rows)
    out_specs = (rows, rows) + (weight,) * 7 + (gain, gain)
    return jax.shard_map(
        on_device, mesh=mesh, in_specs=in_specs, out_specs=out_specs, check_vma=False
    )
```

```python
import functools
import math

import jax
import jax.numpy as jnp
from jax import lax
from jax.experimental import pallas as pl
from jax.experimental.pallas import tpu as pltpu
from jax.sharding import PartitionSpec as P

HEADS = 32
KV_HEADS = 4
HEAD_DIM = 64
PAIR = 2 * HEAD_DIM

EPSILON = 1e-05
THETA = 10000.0
MASKED = -1e30

f32 = jnp.float32
bf16 = jnp.bfloat16

NT = (((1,), (1,)), ((), ()))


def hop(value, bit):
    count = lax.axis_size("seq")
    return lax.ppermute(value, "seq", [(i, i ^ bit) for i in range(count)])


def tie(first, second):
    return lax.optimization_barrier((first, second))


def gather_seq(block, filler=None):
    count = lax.axis_size("seq")
    blocks = [block]
    if count == 2:
        blocks.append(hop(block, 1))
    if count >= 4:
        half = block.shape[0] // 2
        upper, lower = block[:half], block[half:]
        near_upper, other_lower = hop(upper, 1), hop(lower, 2)
        near_lower, other_upper = hop(lower, 1), hop(upper, 2)
        if filler is not None:
            (near_upper, other_lower), filler = tie((near_upper, other_lower), filler)
        far_upper, far_lower = hop(near_upper, 2), hop(other_lower, 1)
        blocks.append(jnp.concatenate([near_upper, near_lower], axis=0))
        blocks.append(jnp.concatenate([other_upper, other_lower], axis=0))
        blocks.append(jnp.concatenate([far_upper, far_lower], axis=0))
    bit = 4
    while bit < count:
        blocks += [hop(one, bit) for one in blocks]
        bit *= 2
    return blocks if filler is None else (blocks, filler)


def gather_direct(block):
    return [block] + [hop(block, r) for r in range(1, lax.axis_size("seq"))]


def add_low(first, second):
    return (first.astype(f32) + second.astype(f32)).astype(bf16)


def scatter_start(parts):
    count = lax.axis_size("seq")
    bit = count // 2
    while bit >= 4:
        there = [hop(parts[bit + r], bit) for r in range(bit)]
        parts = [add_low(parts[r], there[r]) for r in range(bit)]
        bit //= 2
    if count < 4:
        return parts, (), tuple(hop(one, 1) for one in parts[1:])
    half = parts[3].shape[0] // 2
    turning = (hop(parts[3][:half], 1), hop(parts[3][half:], 2))
    straight = (hop(parts[1][:half], 1), hop(parts[2][half:], 2))
    return parts, turning, straight


def scatter_turn(state):
    parts, turning, straight = state
    if not turning:
        return parts[0], (), straight
    half = parts[3].shape[0] // 2
    sent_y = hop(add_low(parts[2][:half], turning[0]), 2)
    sent_x = hop(add_low(parts[1][half:], turning[1]), 1)
    return parts[0], (sent_x, sent_y), straight


def scatter_end(state):
    kept, sent, straight = state
    total = kept.astype(f32)
    if not sent:
        for one in straight:
            total = total + one.astype(f32)
        return total
    total = total + jnp.concatenate([straight[0], sent[0]], axis=0).astype(f32)
    return total + jnp.concatenate([sent[1], straight[1]], axis=0).astype(f32)


def scatter_seq(parts):
    return scatter_end(scatter_turn(scatter_start(parts)))


def rms_scale(values):
    return lax.rsqrt(jnp.mean(values * values, axis=-1, keepdims=True) + EPSILON)


def lane_in_first_half(shape):
    return lax.broadcasted_iota(jnp.int32, shape, 1) < HEAD_DIM


def swap_quarters(values):
    quarter = HEAD_DIM // 2
    lane = lax.broadcasted_iota(jnp.int32, values.shape, 1)
    return jnp.where(
        lane % HEAD_DIM < quarter,
        pltpu.roll(values, PAIR - quarter, 1),
        pltpu.roll(values, quarter, 1),
    )


def project_kernel(width_q, x_ref, gain_ref, w_ref, cos_ref, sin_ref, n_ref, q_ref, k_ref, v_ref):
    values = x_ref[0].astype(f32)
    scale = lax.rsqrt(jnp.mean(values * values, axis=-1, keepdims=True) + EPSILON)
    normed = (values * scale * gain_ref[...].astype(f32)).astype(bf16)
    n_ref[0] = normed
    lin = jnp.dot(normed, w_ref[...], preferred_element_type=f32)
    cosine, sine = cos_ref[0], sin_ref[0]
    for at in range(0, width_q, PAIR):
        part = lin[:, at : at + PAIR]
        turned = (part * cosine + swap_quarters(part) * sine).astype(bf16)
        q_ref[0, :, at : at + PAIR] = (turned.astype(f32) * HEAD_DIM**-0.5).astype(bf16)
    both = lin[:, width_q : width_q + PAIR]
    swapped = pltpu.roll(both, HEAD_DIM, 1)
    first = lane_in_first_half(both.shape)
    keys = jnp.where(first, both, swapped)
    k_ref[0] = (keys * cosine + swap_quarters(keys) * sine).astype(bf16)
    v_ref[0] = jnp.where(first, swapped, both).astype(bf16)


def project(x, gain, weights, cosine, sine, width_q):
    count, rows, width = x.shape
    row_block = lambda last: pl.BlockSpec((1, rows, last), lambda i: (i, 0, 0))
    whole = lambda shape: pl.BlockSpec(shape, lambda i: (0,) * len(shape))
    shape = lambda last: jax.ShapeDtypeStruct((count, rows, last), bf16)
    return pl.pallas_call(
        functools.partial(project_kernel, width_q),
        grid=(count,),
        in_specs=[
            row_block(width),
            whole((1, width)),
            whole((width, width_q + PAIR)),
            row_block(PAIR),
            row_block(PAIR),
        ],
        out_specs=[row_block(width), row_block(width_q), row_block(PAIR), row_block(PAIR)],
        out_shape=[shape(width), shape(width_q), shape(PAIR), shape(PAIR)],
        compiler_params=pltpu.CompilerParams(vmem_limit_bytes=40 * 2**20),
        cost_estimate=pl.CostEstimate(
            flops=2 * count * rows * width * (width_q + PAIR),
            bytes_accessed=6 * count * rows * width,
            transcendentals=0,
        ),
        name="project",
    )(x, gain, weights, cosine, sine)


def take_keys(count, rows, place, k_ref, v_ref, keys_of, values_of):
    for r in range(count):
        at = pl.multiple_of((place ^ r) * rows, rows)
        keys, values = k_ref[r], v_ref[r]
        first = lane_in_first_half(keys.shape)
        zero = jnp.zeros_like(keys)
        keys_of(0, at, jnp.where(first, keys, zero))
        keys_of(1, at, jnp.where(first, zero, keys))
        values_of(0, at, jnp.where(first, values, zero))
        values_of(1, at, jnp.where(first, zero, values))


def attend_kernel(
    count, rows, place_ref, q_ref, k_ref, v_ref, o_ref, l_ref, key_s, value_s, score_s
):
    block = pl.program_id(1)

    @pl.when((pl.program_id(0) == 0) & (block == 0))
    def _():
        def keys_of(h, at, value):
            key_s[h, pl.ds(at, rows), :] = value

        def values_of(h, at, value):
            value_s[h, :, pl.ds(at, rows)] = value.astype(f32).T.astype(bf16)

        take_keys(count, rows, place_ref[0], k_ref, v_ref, keys_of, values_of)

    key_at = lax.broadcasted_iota(jnp.int32, (rows, rows), 0)
    query_at = lax.broadcasted_iota(jnp.int32, (rows, rows), 1)
    allowed = key_at <= query_at

    for c in range(count):

        @pl.when(block == c)
        def _(c=c):
            queries = q_ref[0]
            total = None
            for h in range(2):
                highest = None
                for t in range(c + 1):
                    scores = lax.dot_general(
                        key_s[h, t * rows : (t + 1) * rows, :],
                        queries,
                        NT,
                        preferred_element_type=f32,
                    )
                    if t == c:
                        scores = jnp.where(allowed, scores, MASKED)
                    score_s[h, t * rows : (t + 1) * rows, :] = scores
                    top = jnp.max(scores, axis=0, keepdims=True)
                    highest = top if highest is None else jnp.maximum(highest, top)
                weight = None
                result = None
                for t in range(c + 1):
                    exponent = jnp.exp(score_s[h, t * rows : (t + 1) * rows, :] - highest)
                    one = jnp.sum(exponent, axis=0, keepdims=True)
                    weight = one if weight is None else weight + one
                    part = jnp.dot(
                        value_s[h, :, t * rows : (t + 1) * rows],
                        exponent.astype(bf16),
                        preferred_element_type=f32,
                    )
                    result = part if result is None else result + part
                l_ref[0, 0, h : h + 1, :] = highest + jnp.log(weight)
                result = result / weight
                total = result if total is None else total + result
            o_ref[0] = total.T.astype(bf16)


def attend(place, queries, keys, values):
    count, rows, width = queries.shape
    pairs = width // PAIR
    length = count * rows
    whole = pl.BlockSpec((count, rows, PAIR), lambda p, i, at: (0, 0, 0))
    mine = pl.BlockSpec((1, rows, PAIR), lambda p, i, at: (i ^ at[0], 0, p))
    return pl.pallas_call(
        functools.partial(attend_kernel, count, rows),
        grid_spec=pltpu.PrefetchScalarGridSpec(
            num_scalar_prefetch=1,
            grid=(pairs, count),
            in_specs=[mine, whole, whole],
            out_specs=[mine, pl.BlockSpec((1, 1, 8, rows), lambda p, i, at: (p, i, 0, 0))],
            scratch_shapes=[
                pltpu.VMEM((2, length, PAIR), bf16),
                pltpu.VMEM((2, PAIR, length), bf16),
                pltpu.VMEM((2, length, rows), f32),
            ],
        ),
        out_shape=[
            jax.ShapeDtypeStruct(queries.shape, bf16),
            jax.ShapeDtypeStruct((pairs, count, 8, rows), f32),
        ],
        compiler_params=pltpu.CompilerParams(vmem_limit_bytes=40 * 2**20),
        cost_estimate=pl.CostEstimate(
            flops=4 * pairs * length * length * PAIR,
            bytes_accessed=4 * length * width,
            transcendentals=pairs * length * length,
        ),
        name="attend",
    )(place, queries, keys, values)


def attend_back_kernel(
    count,
    rows,
    place_ref,
    q_ref,
    k_ref,
    v_ref,
    o_ref,
    d_ref,
    l_ref,
    cos_ref,
    sin_ref,
    dq_ref,
    dkv_ref,
    key_s,
    flat_s,
    value_s,
    dk_s,
    dv_s,
):
    pair, block = pl.program_id(0), pl.program_id(1)
    place = place_ref[0]

    @pl.when((pair == 0) & (block == 0))
    def _():
        def keys_of(h, at, value):
            key_s[h, pl.ds(at, rows), :] = value
            flat_s[h, :, pl.ds(at, rows)] = value.astype(f32).T.astype(bf16)

        def values_of(h, at, value):
            value_s[h, pl.ds(at, rows), :] = value

        take_keys(count, rows, place, k_ref, v_ref, keys_of, values_of)
        dk_s[...] = jnp.zeros_like(dk_s)
        dv_s[...] = jnp.zeros_like(dv_s)

    key_at = lax.broadcasted_iota(jnp.int32, (rows, rows), 0)
    query_at = lax.broadcasted_iota(jnp.int32, (rows, rows), 1)
    allowed = key_at <= query_at

    for c in range(count):

        @pl.when(block == c)
        def _(c=c):
            queries, back = q_ref[0], d_ref[0]
            first = lane_in_first_half(queries.shape)
            zero = jnp.zeros_like(queries)
            terms = (back.astype(f32) * o_ref[0].astype(f32)).T
            total = None
            for h in range(2):
                row_term = jnp.sum(
                    terms[h * HEAD_DIM : (h + 1) * HEAD_DIM, :], axis=0, keepdims=True
                )
                query_h = jnp.where(first, queries, zero) if h == 0 else jnp.where(first, zero, queries)
                back_h = jnp.where(first, back, zero) if h == 0 else jnp.where(first, zero, back)
                logsum = l_ref[0, 0, h : h + 1, :]
                for t in range(c + 1):
                    at = slice(t * rows, (t + 1) * rows)
                    scores = lax.dot_general(
                        key_s[h, at, :], queries, NT, preferred_element_type=f32
                    )
                    if t == c:
                        scores = jnp.where(allowed, scores, MASKED)
                    probs = jnp.exp(scores - logsum)
                    back_probs = lax.dot_general(
                        value_s[h, at, :], back, NT, preferred_element_type=f32
                    )
                    back_scores = (probs * (back_probs - row_term)).astype(bf16)
                    dv_s[at, :] += jnp.dot(
                        probs.astype(bf16), back_h, preferred_element_type=f32
                    )
                    dk_s[at, :] += jnp.dot(back_scores, query_h, preferred_element_type=f32)
                    part = jnp.dot(flat_s[h, :, at], back_scores, preferred_element_type=f32)
                    total = part if total is None else total + part
            turned = (total.T * HEAD_DIM**-0.5).astype(bf16).astype(f32)
            dq_ref[0] = (
                turned * cos_ref[block ^ place] - swap_quarters(turned) * sin_ref[block ^ place]
            ).astype(bf16)

    @pl.when((pair == pl.num_programs(0) - 1) & (block == pl.num_programs(1) - 1))
    def _():
        for r in range(count):
            at = pl.multiple_of((place ^ r) * rows, rows)
            keys = dk_s[pl.ds(at, rows), :]
            values = dv_s[pl.ds(at, rows), :]
            keys = (keys + pltpu.roll(keys, HEAD_DIM, 1)).astype(bf16).astype(f32)
            values = values + pltpu.roll(values, HEAD_DIM, 1)
            keys = keys * cos_ref[r] - swap_quarters(keys) * sin_ref[r]
            dkv_ref[r] = jnp.where(lane_in_first_half(keys.shape), keys, values).astype(bf16)


def attend_back(place, queries, keys, values, attended, back, logsum, cosine, sine):
    count, rows, width = queries.shape
    pairs = width // PAIR
    length = count * rows
    whole = pl.BlockSpec((count, rows, PAIR), lambda p, i, at: (0, 0, 0))
    mine = pl.BlockSpec((1, rows, PAIR), lambda p, i, at: (i ^ at[0], 0, p))
    return pl.pallas_call(
        functools.partial(attend_back_kernel, count, rows),
        grid_spec=pltpu.PrefetchScalarGridSpec(
            num_scalar_prefetch=1,
            grid=(pairs, count),
            in_specs=[
                mine,
                whole,
                whole,
                mine,
                mine,
                pl.BlockSpec((1, 1, 8, rows), lambda p, i, at: (p, i, 0, 0)),
                whole,
                whole,
            ],
            out_specs=[mine, whole],
            scratch_shapes=[
                pltpu.VMEM((2, length, PAIR), bf16),
                pltpu.VMEM((2, PAIR, length), bf16),
                pltpu.VMEM((2, length, PAIR), bf16),
                pltpu.VMEM((length, PAIR), f32),
                pltpu.VMEM((length, PAIR), f32),
            ],
        ),
        out_shape=[
            jax.ShapeDtypeStruct(queries.shape, bf16),
            jax.ShapeDtypeStruct((count, rows, PAIR), bf16),
        ],
        compiler_params=pltpu.CompilerParams(vmem_limit_bytes=40 * 2**20),
        cost_estimate=pl.CostEstimate(
            flops=10 * pairs * length * length * PAIR,
            bytes_accessed=8 * length * width,
            transcendentals=pairs * length * length,
        ),
        name="attend_back",
    )(place, queries, keys, values, attended, back, logsum, cosine, sine)


def sort_blocks(place, blocks):
    bit = 1
    while bit < len(blocks):
        flip = (place & bit) != 0
        blocks = [
            jnp.where(flip, blocks[r ^ bit], blocks[r]) for r in range(len(blocks))
        ]
        bit *= 2
    return blocks


def take_columns_kernel(shards, count, piece, place_ref, gate_ref, up_ref, out_ref):
    width = shards * piece
    for c in range(count):

        @pl.when(place_ref[0] == c)
        def _(c=c):
            for at, ref in ((0, gate_ref), (width, up_ref)):
                pieces = []
                for s in range(shards):
                    start = (s * count + c) * piece
                    pieces.append(ref[:, start : start + piece].astype(f32))
                out_ref[:, at : at + width] = jnp.concatenate(pieces, axis=1).astype(bf16)


def take_columns(place, w_gate, w_up, shards, count):
    rows, ff = w_gate.shape
    piece = ff // (shards * count)
    step = min(rows, 128)
    block = lambda last: pl.BlockSpec((step, last), lambda i, at: (i, 0))
    return pl.pallas_call(
        functools.partial(take_columns_kernel, shards, count, piece),
        grid_spec=pltpu.PrefetchScalarGridSpec(
            num_scalar_prefetch=1,
            grid=(rows // step,),
            in_specs=[block(ff), block(ff)],
            out_specs=block(2 * shards * piece),
        ),
        out_shape=jax.ShapeDtypeStruct((rows, 2 * shards * piece), bf16),
        compiler_params=pltpu.CompilerParams(vmem_limit_bytes=40 * 2**20),
        cost_estimate=pl.CostEstimate(
            flops=0, bytes_accessed=6 * rows * ff, transcendentals=0
        ),
        name="take_columns",
    )(place, w_gate, w_up)


def put_columns_kernel(shards, count, piece, place_ref, *refs):
    block_refs = refs[:count]
    gate_w, up_w, gain_ref, gate_ref, up_ref, gain_out = refs[count:]
    width = shards * piece
    blocks = [ref[...].astype(f32) for ref in block_refs]
    blocks = sort_blocks(place_ref[0], blocks)
    total = None
    for at, weight, out in ((0, gate_w, gate_ref), (width, up_w, up_ref)):
        for s in range(shards):
            pieces = [one[:, at + s * piece : at + (s + 1) * piece] for one in blocks]
            joined = jnp.concatenate(pieces, axis=1)
            here = slice(s * count * piece, (s + 1) * count * piece)
            out[:, here] = joined
            term = jnp.sum(joined * weight[:, here].astype(f32), axis=1, keepdims=True)
            total = term if total is None else total + term
    gain_out[...] = jnp.broadcast_to(total, (total.shape[0], 128)).T[:1] / gain_ref[...].astype(f32)


def put_columns(place, blocks, w_gate, w_up, gain, shards):
    count = len(blocks)
    rows, ff = w_gate.shape
    piece = ff // (shards * count)
    step = min(rows, 128)
    block = lambda last: pl.BlockSpec((step, last), lambda i, at: (i, 0))
    flat = pl.BlockSpec((1, step), lambda i, at: (0, i))
    return pl.pallas_call(
        functools.partial(put_columns_kernel, shards, count, piece),
        grid_spec=pltpu.PrefetchScalarGridSpec(
            num_scalar_prefetch=1,
            grid=(rows // step,),
            in_specs=[block(blocks[0].shape[1])] * count + [block(ff), block(ff), flat],
            out_specs=[block(ff), block(ff), flat],
        ),
        out_shape=[
            jax.ShapeDtypeStruct((rows, ff), f32),
            jax.ShapeDtypeStruct((rows, ff), f32),
            jax.ShapeDtypeStruct((1, rows), f32),
        ],
        compiler_params=pltpu.CompilerParams(vmem_limit_bytes=58 * 2**20),
        cost_estimate=pl.CostEstimate(
            flops=0, bytes_accessed=16 * rows * ff, transcendentals=0
        ),
        name="put_columns",
    )(place, *blocks, w_gate, w_up, gain)


def put_attention_kernel(count, copies, width_q, place_ref, *refs):
    block_refs = refs[:count]
    q_w, k_w, v_w, gain_ref, q_ref, k_ref, v_ref, o_ref, gain_out = refs[count:]
    blocks = [ref[...].astype(f32) for ref in block_refs]
    blocks = sort_blocks(place_ref[0], blocks)
    width_o = o_ref.shape[1] // count
    for a in range(count):
        q_ref[:, a * width_q : (a + 1) * width_q] = blocks[a][:, :width_q]
        o_ref[:, a * width_o : (a + 1) * width_o] = blocks[a][:, width_q + PAIR :]
    for part, out in ((0, k_ref), (HEAD_DIM, v_ref)):
        heads = []
        for h in range(count // copies):
            one = None
            for c in range(copies):
                at = width_q + part
                term = blocks[h * copies + c][:, at : at + HEAD_DIM]
                one = term if one is None else one + term
            heads.append(one)
        out[...] = jnp.concatenate(heads, axis=1)
    total = None
    for weight, out in ((q_w, q_ref), (k_w, k_ref), (v_w, v_ref)):
        term = jnp.sum(out[...] * weight[...].astype(f32), axis=1, keepdims=True)
        total = term if total is None else total + term
    gain_out[...] = jnp.broadcast_to(total, (total.shape[0], 128)).T[:1] / gain_ref[...].astype(f32)


def put_attention(place, blocks, w_query, w_key, w_value, gain, width, copies):
    count = len(blocks)
    rows, wide_q = w_query.shape
    wide_k = w_key.shape[1]
    step = min(rows, 128)
    block = lambda last: pl.BlockSpec((step, last), lambda i, at: (i, 0))
    flat = pl.BlockSpec((1, step), lambda i, at: (0, i))
    return pl.pallas_call(
        functools.partial(put_attention_kernel, count, copies, wide_q // count),
        grid_spec=pltpu.PrefetchScalarGridSpec(
            num_scalar_prefetch=1,
            grid=(rows // step,),
            in_specs=[block(blocks[0].shape[1])] * count
            + [block(wide_q), block(wide_k), block(wide_k), flat],
            out_specs=[block(wide_q), block(wide_k), block(wide_k), block(width), flat],
        ),
        out_shape=[
            jax.ShapeDtypeStruct((rows, last), f32) for last in (wide_q, wide_k, wide_k, width)
        ]
        + [jax.ShapeDtypeStruct((1, rows), f32)],
        compiler_params=pltpu.CompilerParams(vmem_limit_bytes=58 * 2**20),
        cost_estimate=pl.CostEstimate(
            flops=0, bytes_accessed=16 * rows * wide_q, transcendentals=0
        ),
        name="put_attention",
    )(place, *blocks, w_query, w_key, w_value, gain)


def on_device(
    tokens, w_query, w_key, w_value, w_out, w_gate, w_up, w_down, gain_attn, gain_mlp, cotangent
):
    count = lax.axis_size("seq")
    shards = lax.axis_size("shard")
    place = lax.axis_index("seq")
    mine = tokens[0]
    rows, width = mine.shape
    length = rows * count
    width_q = HEADS * HEAD_DIM // count
    local_kv = max(1, KV_HEADS // count)
    copies = count * local_kv // KV_HEADS
    width_kv = local_kv * HEAD_DIM
    assert width_kv == HEAD_DIM
    ff = w_gate.shape[1]
    piece = ff // (shards * count)
    width_f = shards * piece
    place_arg = place.reshape(1).astype(jnp.int32)

    def columns(weight, start, size):
        return lax.dynamic_slice_in_dim(weight, start, size, axis=1)

    def from_shards(block):
        return lax.all_gather(block, "shard", axis=0, tiled=True)

    kv_start = (place * local_kv // copies) * HEAD_DIM
    part_d = width // count
    width_qkv = width_q + PAIR
    gains = lax.all_gather(jnp.stack([gain_attn, gain_mlp]), "shard", axis=1, tiled=True)
    gain_first, gain_second = gains[0:1], gains[1:2].astype(f32)
    w_attn = from_shards(
        jnp.concatenate(
            [
                columns(w_query, place * width_q, width_q),
                columns(w_key, kv_start, width_kv),
                columns(w_value, kv_start, width_kv),
                columns(w_out, place * part_d, part_d),
            ],
            axis=1,
        )
    )
    input_blocks, (gate_in, up_in) = gather_seq(mine, (w_gate, w_up))
    w_gu = from_shards(take_columns(place_arg, gate_in, up_in, shards, count))
    w_dn = from_shards(lax.dynamic_slice_in_dim(w_down, place * piece, piece, axis=0))
    inputs = jnp.stack(input_blocks)

    blocks_at = place ^ jnp.arange(count)
    positions = (blocks_at[:, None] * rows + jnp.arange(rows)[None, :]).astype(f32)
    half_dim = HEAD_DIM // 2
    lanes = jnp.arange(PAIR)
    frequency = jnp.exp(-math.log(THETA) * (lanes % half_dim).astype(f32) * 2.0 / HEAD_DIM)
    angles = positions[:, :, None] * frequency
    cosine = jnp.cos(angles)
    sine = jnp.sin(angles) * jnp.where(lanes % HEAD_DIM < half_dim, -1.0, 1.0)

    normed, queries, keys, values = project(inputs, gain_first, w_attn, cosine, sine, width_q)
    w_attn, queries = tie(w_attn, queries)
    w_qkv, w_o_columns = w_attn[:, :width_qkv], w_attn[:, width_qkv:]

    w_o = jnp.zeros((width_q, width), bf16)
    for r in range(count):
        rows_r = lax.dynamic_slice_in_dim(w_o_columns, (place ^ r) * width_q, width_q, axis=0)
        rows_r = hop(rows_r, r) if r else rows_r
        w_o = lax.dynamic_update_slice_in_dim(w_o, rows_r, (place ^ r) * part_d, axis=1)

    attended, logsum = attend(place_arg, queries, keys, values)
    attended_rows = attended.reshape(length, width_q)

    def split(array):
        array = array.astype(bf16)
        return [array[r * rows : (r + 1) * rows] for r in range(count)]

    def token_sum(left, right):
        return jnp.einsum("tf,td->fd", left, right, preferred_element_type=f32).astype(bf16)

    def to_owners(part):
        return lax.psum_scatter(part, "shard", scatter_dimension=0, tiled=True)

    def norm_back(values_in, scale, gain, back):
        branch = back * gain
        return scale * (
            branch - values_in * scale * scale * jnp.mean(branch * values_in, -1, keepdims=True)
        )

    middle = mine.astype(f32) + scatter_seq(
        split(jnp.dot(attended_rows, w_o, preferred_element_type=f32))
    )
    scale_mid = rms_scale(middle)
    normed_blocks = gather_seq((middle * scale_mid * gain_second).astype(bf16))
    normed_blocks, cot = tie(normed_blocks, cotangent[0])
    normed_mlp = jnp.concatenate(normed_blocks)
    gate_up = jnp.dot(normed_mlp, w_gu, preferred_element_type=f32)
    back_blocks, gate_up = gather_seq(cot, gate_up)
    back_mlp = jnp.concatenate(back_blocks)

    gate_lin, upward = gate_up[:, :width_f], gate_up[:, width_f:]
    sigmoid_gate = jax.nn.sigmoid(gate_lin)
    silu_gate = gate_lin * sigmoid_gate
    hidden = (silu_gate * upward).astype(bf16)
    down_part = token_sum(hidden, back_mlp)
    own_down = to_owners(down_part)

    w_dn, down_part = tie(w_dn, down_part)
    out_parts = split(jnp.dot(hidden, w_dn, preferred_element_type=f32))
    w_dn, out_parts = tie(w_dn, out_parts)
    kept, turning, straight = scatter_start(out_parts)
    back_hidden = (
        jnp.einsum("td,fd->tf", back_mlp, w_dn, preferred_element_type=f32).astype(bf16).astype(f32)
    )
    back_gate = back_hidden * upward * sigmoid_gate * (1.0 + gate_lin * (1.0 - sigmoid_gate))
    back_up = back_hidden * silu_gate
    back_gu = jnp.concatenate([back_gate.astype(bf16), back_up.astype(bf16)], axis=1)

    turning, back_gu = tie(turning, back_gu)
    kept, sent, straight = scatter_turn((kept, turning, straight))

    parts = split(jnp.einsum("tf,df->td", back_gu, w_gu, preferred_element_type=f32))
    parts, (sent, straight) = tie(parts, (sent, straight))
    output = (middle + scatter_end((kept, sent, straight))).astype(bf16)[None]
    parts, turning, straight = scatter_start(parts)
    gu_part = token_sum(normed_mlp, back_gu)
    (turning, straight), gu_part = tie((turning, straight), gu_part)
    back_normed_mlp = scatter_end(scatter_turn((parts, turning, straight)))
    own_gu = to_owners(gu_part)

    back_middle = cot.astype(f32) + norm_back(middle, scale_mid, gain_second, back_normed_mlp)
    back_blocks = gather_seq(back_middle.astype(bf16))
    back_blocks, own_down = tie(back_blocks, own_down)
    back_branch = jnp.concatenate(back_blocks)

    back_attended = jnp.einsum("td,qd->tq", back_branch, w_o, preferred_element_type=f32)
    back_attended = back_attended.astype(bf16).reshape(count, rows, width_q)
    out_part = token_sum(attended_rows, back_branch)
    out_blocks = []
    for r in range(count):
        part_r = lax.dynamic_slice_in_dim(out_part, (place ^ r) * part_d, part_d, axis=1)
        out_blocks.append(hop(part_r, r) if r else part_r)
    down_blocks = gather_direct(own_down)
    back_query, back_kv = attend_back(
        place_arg, queries, keys, values, attended, back_attended, logsum, cosine, sine
    )
    back_query, (out_blocks, down_blocks) = tie(back_query, (out_blocks, down_blocks))
    back_qkv = jnp.concatenate([back_query, back_kv], axis=2).reshape(length, -1)

    attn_part = jnp.pad(
        token_sum(normed.reshape(length, width), back_qkv), ((0, 0), (0, part_d))
    )
    for r in range(count):
        attn_part = lax.dynamic_update_slice(
            attn_part, out_blocks[r], ((place ^ r) * width_q, width_qkv)
        )
    attn_part, own_gu = tie(attn_part, own_gu)
    own_attn = to_owners(attn_part)

    parts = split(jnp.einsum("tq,dq->td", back_qkv, w_qkv, preferred_element_type=f32))
    back_normed = scatter_seq(parts)
    back_normed, own_gu = tie(back_normed, own_gu)
    mine_in = mine.astype(f32)
    grad_tokens = back_middle + norm_back(
        mine_in, rms_scale(mine_in), gain_first.astype(f32), back_normed
    )

    grad_down = jnp.zeros((count * piece, width), f32)
    for r, block in enumerate(down_blocks):
        grad_down = lax.dynamic_update_slice_in_dim(
            grad_down, block.astype(f32), (place ^ r) * piece, axis=0
        )
    grad_gate, grad_up, grad_gain_mlp = put_columns(
        place_arg, gather_seq(own_gu), w_gate, w_up, gain_mlp.reshape(1, -1), shards
    )
    grad_query, grad_key, grad_value, grad_out, grad_gain_attn = put_attention(
        place_arg,
        gather_seq(own_attn),
        w_query,
        w_key,
        w_value,
        gain_attn.reshape(1, -1),
        width,
        copies,
    )
    return (
        output,
        grad_tokens[None],
        grad_query,
        grad_key,
        grad_value,
        grad_out,
        grad_gate,
        grad_up,
        grad_down,
        grad_gain_attn.reshape(-1),
        grad_gain_mlp.reshape(-1),
    )


def solution(mesh):
    rows = P("shard", "seq", None)
    weight = P("shard", None)
    gain = P("shard")
    in_specs = (rows,) + (weight,) * 7 + (gain, gain, rows)
    out_specs = (rows, rows) + (weight,) * 7 + (gain, gain)
    return jax.shard_map(
        on_device, mesh=mesh, in_specs=in_specs, out_specs=out_specs, check_vma=False
    )
```

```python
import functools
import math

import jax
import jax.numpy as jnp
from jax import lax
from jax.experimental import pallas as pl
from jax.experimental.pallas import tpu as pltpu
from jax.sharding import PartitionSpec as P

HEADS = 32
KV_HEADS = 4
HEAD_DIM = 64
PAIR = 2 * HEAD_DIM

EPSILON = 1e-05
THETA = 10000.0
MASKED = -1e30
MIB = 2**20

f32 = jnp.float32
bf16 = jnp.bfloat16

NT = (((1,), (1,)), ((), ()))


def hop(value, bit):
    count = lax.axis_size("seq")
    return lax.ppermute(value, "seq", [(i, i ^ bit) for i in range(count)])


def tie(first, second):
    return lax.optimization_barrier((first, second))


def gather_seq(block, filler=None):
    count = lax.axis_size("seq")
    pieces = block if isinstance(block, tuple) else None
    if pieces is not None:
        block = jnp.concatenate(pieces, axis=0)
    blocks = [block]
    if count == 2:
        blocks.append(hop(block, 1))
    if count >= 4:
        half = block.shape[0] // 2
        upper, lower = pieces or (block[:half], block[half:])
        near_upper, other_lower = hop(upper, 1), hop(lower, 2)
        near_lower, other_upper = hop(lower, 1), hop(upper, 2)
        if filler is not None:
            (near_upper, other_lower), filler = tie((near_upper, other_lower), filler)
        far_upper, far_lower = hop(near_upper, 2), hop(other_lower, 1)
        blocks.append(jnp.concatenate([near_upper, near_lower], axis=0))
        blocks.append(jnp.concatenate([other_upper, other_lower], axis=0))
        blocks.append(jnp.concatenate([far_upper, far_lower], axis=0))
    bit = 4
    while bit < count:
        blocks += [hop(one, bit) for one in blocks]
        bit *= 2
    return blocks if filler is None else (blocks, filler)


def gather_halves(upper, lower):
    if lax.axis_size("seq") != 4:
        return gather_seq(jnp.concatenate([upper, lower], axis=0))
    near_upper, other_lower = hop(upper, 1), hop(lower, 2)
    near_lower, other_upper = hop(lower, 1), hop(upper, 2)
    far_upper, far_lower = hop(near_upper, 2), hop(other_lower, 1)
    return [upper, lower, near_upper, near_lower, other_upper, other_lower, far_upper, far_lower]


def gather_near(block):
    return (hop(block, 1), hop(block, 2)) if lax.axis_size("seq") == 4 else ()


def gather_far(block, near):
    if not near:
        return gather_seq(block), ()
    half = block.shape[0] // 2
    return [block, *near], (hop(near[0][:half], 2), hop(near[1][half:], 1))


def add_low(first, second):
    return (first.astype(f32) + second.astype(f32)).astype(bf16)


def scatter_start(parts):
    count = lax.axis_size("seq")
    bit = count // 2
    while bit >= 4:
        there = [hop(parts[bit + r], bit) for r in range(bit)]
        parts = [add_low(parts[r], there[r]) for r in range(bit)]
        bit //= 2
    if count < 4:
        return parts, (), tuple(hop(one, 1) for one in parts[1:])
    half = parts[3].shape[0] // 2
    turning = (hop(parts[3][:half], 1), hop(parts[3][half:], 2))
    straight = (hop(parts[1][:half], 1), hop(parts[2][half:], 2))
    return parts, turning, straight


def scatter_turn(state):
    parts, turning, straight = state
    if not turning:
        return parts[0], (), straight
    half = parts[3].shape[0] // 2
    sent_y = hop(add_low(parts[2][:half], turning[0]), 2)
    sent_x = hop(add_low(parts[1][half:], turning[1]), 1)
    return parts[0], (sent_x, sent_y), straight


def scatter_pieces(state):
    kept, sent, straight = state
    if not sent:
        return scatter_end(state), ()
    return kept, (straight[0], sent[0], sent[1], straight[1])


def scatter_end(state):
    kept, sent, straight = state
    total = kept.astype(f32)
    if not sent:
        for one in straight:
            total = total + one.astype(f32)
        return total
    total = total + jnp.concatenate([straight[0], sent[0]], axis=0).astype(f32)
    return total + jnp.concatenate([sent[1], straight[1]], axis=0).astype(f32)


def scatter_seq(parts):
    return scatter_end(scatter_turn(scatter_start(parts)))


def rms_scale(values):
    return lax.rsqrt(jnp.mean(values * values, axis=-1, keepdims=True) + EPSILON)


def lane_in_first_half(shape):
    return lax.broadcasted_iota(jnp.int32, shape, 1) < HEAD_DIM


def swap_quarters(values):
    quarter = HEAD_DIM // 2
    lane = lax.broadcasted_iota(jnp.int32, values.shape, 1)
    return jnp.where(
        lane % HEAD_DIM < quarter,
        pltpu.roll(values, PAIR - quarter, 1),
        pltpu.roll(values, quarter, 1),
    )


def branch_kernel(count, given, place_ref, w_ref, t_ref, *refs):
    back_ref, out_refs, rows_s = refs[given], refs[given + 1 : -1], refs[-1]
    step = pl.program_id(0)

    @pl.when(step == 0)
    def _():
        at = 0
        for ref in refs[:given]:
            rows_s[at : at + ref.shape[0], :] = ref[...]
            at += ref.shape[0]

    rows = rows_s.shape[0] // count
    part = rows_s.shape[1] // count
    block = rows_s[pl.ds(pl.multiple_of(step * rows, rows), rows), :]
    back_ref[0] = lax.dot_general(
        block, w_ref[...], NT, preferred_element_type=f32
    ).astype(bf16)
    columns = rows_s[:, pl.ds(pl.multiple_of(step * part, part), part)]
    result = jnp.dot(t_ref[...], columns, preferred_element_type=f32).astype(bf16)
    for r in range(count):

        @pl.when(step == place_ref[0] ^ r)
        def _(r=r):
            out_refs[r][...] = result


def branch(place, pieces, w_o, attended_t):
    count = lax.axis_size("seq")
    width_q, length = attended_t.shape
    width = w_o.shape[1]
    rows, part = length // count, width // count
    whole = lambda shape: pl.BlockSpec(shape, lambda i, at: (0,) * len(shape))
    return pl.pallas_call(
        functools.partial(branch_kernel, count, len(pieces)),
        grid_spec=pltpu.PrefetchScalarGridSpec(
            num_scalar_prefetch=1,
            grid=(count,),
            in_specs=[whole(w_o.shape), whole(attended_t.shape)]
            + [whole(one.shape) for one in pieces],
            out_specs=[pl.BlockSpec((1, rows, width_q), lambda i, at: (i, 0, 0))]
            + [whole((width_q, part))] * count,
            scratch_shapes=[pltpu.VMEM((length, width), bf16)],
        ),
        out_shape=[jax.ShapeDtypeStruct((count, rows, width_q), bf16)]
        + [jax.ShapeDtypeStruct((width_q, part), bf16)] * count,
        compiler_params=pltpu.CompilerParams(vmem_limit_bytes=60 * MIB),
        cost_estimate=pl.CostEstimate(flops=1, bytes_accessed=1, transcendentals=0),
        name="branch",
    )(place, w_o, attended_t, *pieces)


def attention_grads_kernel(count, place_ref, n_ref, dq_ref, dkv_ref, *refs):
    out_refs, part_ref, sorted_s = refs[:count], refs[count], refs[count + 1]

    @pl.when(pl.program_id(0) == 0)
    def _():
        for r in range(count):
            sorted_s[place_ref[0] ^ r] = out_refs[r][...]

    def token_sum(left, right):
        return lax.dot_general(
            left, right, (((0,), (0,)), ((), ())), preferred_element_type=f32
        ).astype(bf16)

    width_q = dq_ref.shape[1]
    normed = n_ref[...]
    part_ref[:, :width_q] = token_sum(normed, dq_ref[...])
    part_ref[:, width_q : width_q + PAIR] = token_sum(normed, dkv_ref[...])
    part_ref[:, width_q + PAIR :] = sorted_s[pl.program_id(0)]


def attention_grads(place, normed, back_query, back_kv, out_blocks):
    count = len(out_blocks)
    length, width = normed.shape
    width_q = back_query.shape[1]
    part_q, part_d = out_blocks[0].shape
    whole = lambda shape: pl.BlockSpec(shape, lambda a, at: (0, 0))
    wide = width_q + PAIR + part_d
    return pl.pallas_call(
        functools.partial(attention_grads_kernel, count),
        grid_spec=pltpu.PrefetchScalarGridSpec(
            num_scalar_prefetch=1,
            grid=(count,),
            in_specs=[
                pl.BlockSpec((length, part_q), lambda a, at: (0, a)),
                whole((length, width_q)),
                whole((length, PAIR)),
            ]
            + [whole((part_q, part_d))] * count,
            out_specs=pl.BlockSpec((part_q, wide), lambda a, at: (a, 0)),
            scratch_shapes=[pltpu.VMEM((count, part_q, part_d), bf16)],
        ),
        out_shape=jax.ShapeDtypeStruct((width, wide), bf16),
        compiler_params=pltpu.CompilerParams(vmem_limit_bytes=60 * MIB),
        cost_estimate=pl.CostEstimate(flops=1, bytes_accessed=1, transcendentals=0),
        name="attention_grads",
    )(place, normed, back_query, back_kv, *out_blocks)


def input_grads_kernel(count, dq_ref, dkv_ref, w_ref, *outs):
    width_q = dq_ref.shape[1]
    weights = w_ref[...]
    result = lax.dot_general(
        dq_ref[...], weights[:, :width_q], NT, preferred_element_type=f32
    ) + lax.dot_general(dkv_ref[...], weights[:, width_q:], NT, preferred_element_type=f32)
    at = 0
    for out in outs:
        out[...] = result[at : at + out.shape[0], :].astype(bf16)
        at += out.shape[0]


def input_grads(back_query, back_kv, weights):
    count = lax.axis_size("seq")
    length, width_q = back_query.shape
    width = weights.shape[0]
    rows = length // count
    sizes = [rows] * (count - 1) + ([rows // 2] * 2 if count == 4 else [rows])
    step = 512
    whole = lambda shape: pl.BlockSpec(shape, lambda i: (0, 0))
    return pl.pallas_call(
        functools.partial(input_grads_kernel, count),
        grid=(width // step,),
        in_specs=[
            whole(back_query.shape),
            whole(back_kv.shape),
            pl.BlockSpec((step, width_q + PAIR), lambda i: (i, 0)),
        ],
        out_specs=[pl.BlockSpec((size, step), lambda i: (0, i)) for size in sizes],
        out_shape=[jax.ShapeDtypeStruct((size, width), bf16) for size in sizes],
        compiler_params=pltpu.CompilerParams(vmem_limit_bytes=40 * MIB),
        cost_estimate=pl.CostEstimate(flops=1, bytes_accessed=1, transcendentals=0),
        name="input_grads",
    )(back_query, back_kv, weights)


def turn_kernel(x_ref, y_ref, upper_ref, lower_ref, to_x_ref, to_y_ref):
    first = pl.program_id(0) == 0
    to_x, to_y = x_ref[...].astype(f32), y_ref[...].astype(f32)
    to_x_ref[...] = jnp.where(first, to_x, to_x + lower_ref[...].astype(f32)).astype(bf16)
    to_y_ref[...] = jnp.where(first, to_y + upper_ref[...].astype(f32), to_y).astype(bf16)


def turn(parts, turning):
    half, width = turning[0].shape
    part = pl.BlockSpec((half, width), lambda i: (i, 0))
    fixed = pl.BlockSpec((half, width), lambda i: (0, 0))
    return pl.pallas_call(
        turn_kernel,
        grid=(2,),
        in_specs=[part, part, fixed, fixed],
        out_specs=[part, part],
        out_shape=[jax.ShapeDtypeStruct((2 * half, width), bf16)] * 2,
        compiler_params=pltpu.CompilerParams(vmem_limit_bytes=60 * MIB),
        cost_estimate=pl.CostEstimate(flops=1, bytes_accessed=1, transcendentals=0),
        name="turn",
    )(*parts, *turning)


def norm_kernel(given, kept, add_ref, gain_ref, *refs):
    arrived, (middle_ref, upper_ref, lower_ref) = refs[:given], refs[given:]
    first = 2 * pl.program_id(0) < pl.num_programs(0)
    values = kept[...].astype(f32) + add_ref[...].astype(f32)
    if given == 4:
        for upper, lower in (arrived[:2], arrived[2:]):
            values += jnp.where(first, upper[...].astype(f32), lower[...].astype(f32))
    middle_ref[...] = values
    scale = lax.rsqrt(jnp.mean(values * values, axis=-1, keepdims=True) + EPSILON)
    result = (values * scale * gain_ref[...].astype(f32)).astype(bf16)

    @pl.when(first)
    def _():
        upper_ref[...] = result

    @pl.when(jnp.logical_not(first))
    def _():
        lower_ref[...] = result


def norm(kept, arrived, add, gain):
    rows, width = add.shape
    half = rows // 2
    step = half // 2
    block = pl.BlockSpec((step, width), lambda i: (i, 0))
    fixed = pl.BlockSpec((1, width), lambda i: (0, 0))
    upper = pl.BlockSpec((step, width), lambda i: (jnp.minimum(i, 1), 0))
    lower = pl.BlockSpec((step, width), lambda i: (jnp.maximum(i, 2) - 2, 0))
    pieces = [upper, lower] * 2 if len(arrived) == 4 else [block] * len(arrived)
    low = jax.ShapeDtypeStruct((half, width), bf16)
    return pl.pallas_call(
        functools.partial(norm_kernel, len(arrived)),
        grid=(4,),
        in_specs=[block, block, fixed] + pieces,
        out_specs=[block, upper, lower],
        out_shape=[jax.ShapeDtypeStruct((rows, width), f32), low, low],
        compiler_params=pltpu.CompilerParams(vmem_limit_bytes=60 * MIB),
        cost_estimate=pl.CostEstimate(flops=1, bytes_accessed=1, transcendentals=0),
        name="norm",
    )(kept, add, gain, *arrived)


def norm_back_kernel(given, *refs):
    kept, values_ref, add_ref, gain_ref = refs[:4]
    arrived, outs = refs[4 : 4 + given], refs[4 + given :]
    back = kept[...].astype(f32)
    first = 2 * pl.program_id(0) < pl.num_programs(0)
    if given == 2:
        back += arrived[0][...].astype(f32) + arrived[1][...].astype(f32)
    if given == 4:
        for upper, lower in (arrived[:2], arrived[2:]):
            back += jnp.where(first, upper[...].astype(f32), lower[...].astype(f32))
    values = values_ref[...].astype(f32)
    branch = back * gain_ref[...].astype(f32)
    scale = lax.rsqrt(jnp.mean(values * values, axis=-1, keepdims=True) + EPSILON)
    inner = jnp.mean(branch * values, axis=-1, keepdims=True)
    result = add_ref[...].astype(f32) + scale * (branch - values * (scale * scale * inner))
    outs[0][...] = result
    if len(outs) == 3:

        @pl.when(first)
        def _():
            outs[1][...] = result.astype(bf16)

        @pl.when(jnp.logical_not(first))
        def _():
            outs[2][...] = result.astype(bf16)


def norm_back(kept, arrived, values, add, gain, halves):
    rows, width = values.shape
    half = rows // 2
    step = half // 2
    block = pl.BlockSpec((step, width), lambda i: (i, 0))
    fixed = pl.BlockSpec((1, width), lambda i: (0, 0))
    upper = pl.BlockSpec((step, width), lambda i: (jnp.minimum(i, 1), 0))
    lower = pl.BlockSpec((step, width), lambda i: (jnp.maximum(i, 2) - 2, 0))
    pieces = [upper, lower] * 2 if len(arrived) == 4 else [block] * len(arrived)
    low = jax.ShapeDtypeStruct((half, width), bf16)
    return pl.pallas_call(
        functools.partial(norm_back_kernel, len(arrived)),
        grid=(4,),
        in_specs=[block, block, block, fixed] + pieces,
        out_specs=[block] + ([upper, lower] if halves else []),
        out_shape=[jax.ShapeDtypeStruct((rows, width), f32)] + [low] * (2 if halves else 0),
        compiler_params=pltpu.CompilerParams(vmem_limit_bytes=60 * MIB),
        cost_estimate=pl.CostEstimate(flops=1, bytes_accessed=1, transcendentals=0),
        name="norm_back",
    )(kept, values, add, gain, *arrived)


def spread_blocks(count, refs, store):
    for r in range(count):
        if r == count - 1 and len(refs) > count:
            store(r, 0, refs[r])
            store(r, refs[r].shape[0], refs[r + 1])
        else:
            store(r, 0, refs[r])


def project_kernel(count, width_q, given, *refs):
    gain_ref, w_ref, cos_ref, sin_ref, n_ref, q_ref, k_ref, v_ref, x_s = refs[given:]

    def store(r, at, ref):
        @pl.when(pl.program_id(0) == r)
        def _():
            x_s[at : at + ref.shape[0], :] = ref[...]

    spread_blocks(count, refs[:given], store)
    values = x_s[...].astype(f32)
    scale = lax.rsqrt(jnp.mean(values * values, axis=-1, keepdims=True) + EPSILON)
    normed = (values * scale * gain_ref[...].astype(f32)).astype(bf16)
    n_ref[0] = normed
    lin = jnp.dot(normed, w_ref[...], preferred_element_type=f32)
    cosine, sine = cos_ref[0], sin_ref[0]
    for at in range(0, width_q, PAIR):
        part = lin[:, at : at + PAIR]
        turned = (part * cosine + swap_quarters(part) * sine).astype(bf16)
        q_ref[0, :, at : at + PAIR] = (turned.astype(f32) * HEAD_DIM**-0.5).astype(bf16)
    both = lin[:, width_q : width_q + PAIR]
    swapped = pltpu.roll(both, HEAD_DIM, 1)
    first = lane_in_first_half(both.shape)
    keys = jnp.where(first, both, swapped)
    k_ref[0] = (keys * cosine + swap_quarters(keys) * sine).astype(bf16)
    v_ref[0] = jnp.where(first, swapped, both).astype(bf16)


def project(blocks, gain, weights, cosine, sine, width_q):
    count = lax.axis_size("seq")
    rows, width = blocks[0].shape
    row_block = lambda last: pl.BlockSpec((1, rows, last), lambda i: (i, 0, 0))
    whole = lambda shape: pl.BlockSpec(shape, lambda i: (0,) * len(shape))
    shape = lambda last: jax.ShapeDtypeStruct((count, rows, last), bf16)
    return pl.pallas_call(
        functools.partial(project_kernel, count, width_q, len(blocks)),
        grid=(count,),
        in_specs=[whole(one.shape) for one in blocks]
        + [
            whole((1, width)),
            whole((width, width_q + PAIR)),
            row_block(PAIR),
            row_block(PAIR),
        ],
        out_specs=[row_block(width), row_block(width_q), row_block(PAIR), row_block(PAIR)],
        out_shape=[shape(width), shape(width_q), shape(PAIR), shape(PAIR)],
        scratch_shapes=[pltpu.VMEM((rows, width), bf16)],
        compiler_params=pltpu.CompilerParams(vmem_limit_bytes=60 * MIB),
        cost_estimate=pl.CostEstimate(flops=1, bytes_accessed=1, transcendentals=0),
        name="project",
    )(*blocks, gain, weights, cosine, sine)


def take_keys(count, rows, place, k_ref, v_ref, keys_of, values_of):
    for r in range(count):
        at = pl.multiple_of((place ^ r) * rows, rows)
        keys, values = k_ref[r], v_ref[r]
        first = lane_in_first_half(keys.shape)
        zero = jnp.zeros_like(keys)
        keys_of(0, at, jnp.where(first, keys, zero))
        keys_of(1, at, jnp.where(first, zero, keys))
        values_of(0, at, jnp.where(first, values, zero))
        values_of(1, at, jnp.where(first, zero, values))


def attend_kernel(
    count, rows, place_ref, q_ref, k_ref, v_ref, o_ref, t_ref, l_ref, key_s, value_s, score_s
):
    block = pl.program_id(1)

    @pl.when((pl.program_id(0) == 0) & (block == 0))
    def _():
        def keys_of(h, at, value):
            key_s[h, pl.ds(at, rows), :] = value

        def values_of(h, at, value):
            value_s[h, :, pl.ds(at, rows)] = value.astype(f32).T.astype(bf16)

        take_keys(count, rows, place_ref[0], k_ref, v_ref, keys_of, values_of)

    key_at = lax.broadcasted_iota(jnp.int32, (rows, rows), 0)
    query_at = lax.broadcasted_iota(jnp.int32, (rows, rows), 1)
    allowed = key_at <= query_at

    for c in range(count):

        @pl.when(block == c)
        def _(c=c):
            queries = q_ref[0]
            total = None
            for h in range(2):
                highest = None
                for t in range(c + 1):
                    scores = lax.dot_general(
                        key_s[h, t * rows : (t + 1) * rows, :],
                        queries,
                        NT,
                        preferred_element_type=f32,
                    )
                    if t == c:
                        scores = jnp.where(allowed, scores, MASKED)
                    score_s[h, t * rows : (t + 1) * rows, :] = scores
                    top = jnp.max(scores, axis=0, keepdims=True)
                    highest = top if highest is None else jnp.maximum(highest, top)
                weight = None
                result = None
                for t in range(c + 1):
                    exponent = jnp.exp(score_s[h, t * rows : (t + 1) * rows, :] - highest)
                    one = jnp.sum(exponent, axis=0, keepdims=True)
                    weight = one if weight is None else weight + one
                    part = jnp.dot(
                        value_s[h, :, t * rows : (t + 1) * rows],
                        exponent.astype(bf16),
                        preferred_element_type=f32,
                    )
                    result = part if result is None else result + part
                l_ref[0, 0, h : h + 1, :] = highest + jnp.log(weight)
                result = result / weight
                total = result if total is None else total + result
            o_ref[0] = total.T.astype(bf16)
            t_ref[...] = total.astype(bf16)


def attend(place, queries, keys, values):
    count, rows, width = queries.shape
    pairs = width // PAIR
    length = count * rows
    whole = pl.BlockSpec((count, rows, PAIR), lambda p, i, at: (0, 0, 0))
    mine = pl.BlockSpec((1, rows, PAIR), lambda p, i, at: (i ^ at[0], 0, p))
    return pl.pallas_call(
        functools.partial(attend_kernel, count, rows),
        grid_spec=pltpu.PrefetchScalarGridSpec(
            num_scalar_prefetch=1,
            grid=(pairs, count),
            in_specs=[mine, whole, whole],
            out_specs=[
                mine,
                pl.BlockSpec((PAIR, rows), lambda p, i, at: (p, i ^ at[0])),
                pl.BlockSpec((1, 1, 8, rows), lambda p, i, at: (p, i, 0, 0)),
            ],
            scratch_shapes=[
                pltpu.VMEM((2, length, PAIR), bf16),
                pltpu.VMEM((2, PAIR, length), bf16),
                pltpu.VMEM((2, length, rows), f32),
            ],
        ),
        out_shape=[
            jax.ShapeDtypeStruct(queries.shape, bf16),
            jax.ShapeDtypeStruct((width, length), bf16),
            jax.ShapeDtypeStruct((pairs, count, 8, rows), f32),
        ],
        compiler_params=pltpu.CompilerParams(vmem_limit_bytes=24 * MIB),
        cost_estimate=pl.CostEstimate(flops=1, bytes_accessed=1, transcendentals=0),
        name="attend",
    )(place, queries, keys, values)


def attend_back_kernel(
    count,
    rows,
    place_ref,
    q_ref,
    k_ref,
    v_ref,
    o_ref,
    d_ref,
    l_ref,
    cos_ref,
    sin_ref,
    dq_ref,
    dkv_ref,
    key_s,
    flat_s,
    value_s,
    dk_s,
    dv_s,
):
    pair = pl.program_id(0)
    place = place_ref[0]

    @pl.when(pair == 0)
    def _():
        def keys_of(h, at, value):
            key_s[h, pl.ds(at, rows), :] = value
            flat_s[h, :, pl.ds(at, rows)] = value.astype(f32).T.astype(bf16)

        def values_of(h, at, value):
            value_s[h, pl.ds(at, rows), :] = value

        take_keys(count, rows, place, k_ref, v_ref, keys_of, values_of)
        dk_s[...] = jnp.zeros_like(dk_s)
        dv_s[...] = jnp.zeros_like(dv_s)

    key_at = lax.broadcasted_iota(jnp.int32, (rows, rows), 0)
    query_at = lax.broadcasted_iota(jnp.int32, (rows, rows), 1)
    allowed = key_at <= query_at

    for c in range(count):
        block = place ^ c
        queries, back = q_ref[block], d_ref[block]
        first = lane_in_first_half(queries.shape)
        zero = jnp.zeros_like(queries)
        terms = (back.astype(f32) * o_ref[block].astype(f32)).T
        total = None
        for h in range(2):
            row_term = jnp.sum(terms[h * HEAD_DIM : (h + 1) * HEAD_DIM, :], axis=0, keepdims=True)
            query_h = jnp.where(first, queries, zero) if h == 0 else jnp.where(first, zero, queries)
            back_h = jnp.where(first, back, zero) if h == 0 else jnp.where(first, zero, back)
            logsum = l_ref[0, c, h : h + 1, :]
            for t in range(c + 1):
                at = slice(t * rows, (t + 1) * rows)
                scores = lax.dot_general(
                    key_s[h, at, :], queries, NT, preferred_element_type=f32
                )
                if t == c:
                    scores = jnp.where(allowed, scores, MASKED)
                probs = jnp.exp(scores - logsum)
                back_probs = lax.dot_general(
                    value_s[h, at, :], back, NT, preferred_element_type=f32
                )
                back_scores = (probs * (back_probs - row_term)).astype(bf16)
                dv_s[at, :] += jnp.dot(probs.astype(bf16), back_h, preferred_element_type=f32)
                dk_s[at, :] += jnp.dot(back_scores, query_h, preferred_element_type=f32)
                part = jnp.dot(flat_s[h, :, at], back_scores, preferred_element_type=f32)
                total = part if total is None else total + part
        turned = (total.T * HEAD_DIM**-0.5).astype(bf16).astype(f32)
        dq_ref[block] = (
            turned * cos_ref[block] - swap_quarters(turned) * sin_ref[block]
        ).astype(bf16)

    @pl.when(pair == pl.num_programs(0) - 1)
    def _():
        for r in range(count):
            at = pl.multiple_of((place ^ r) * rows, rows)
            keys = dk_s[pl.ds(at, rows), :]
            values = dv_s[pl.ds(at, rows), :]
            keys = (keys + pltpu.roll(keys, HEAD_DIM, 1)).astype(bf16).astype(f32)
            values = values + pltpu.roll(values, HEAD_DIM, 1)
            keys = keys * cos_ref[r] - swap_quarters(keys) * sin_ref[r]
            dkv_ref[r] = jnp.where(lane_in_first_half(keys.shape), keys, values).astype(bf16)


def attend_back(place, queries, keys, values, attended, back, logsum, cosine, sine):
    count, rows, width = queries.shape
    pairs = width // PAIR
    length = count * rows
    whole = pl.BlockSpec((count, rows, PAIR), lambda p, at: (0, 0, 0))
    mine = pl.BlockSpec((count, rows, PAIR), lambda p, at: (0, 0, p))
    return pl.pallas_call(
        functools.partial(attend_back_kernel, count, rows),
        grid_spec=pltpu.PrefetchScalarGridSpec(
            num_scalar_prefetch=1,
            grid=(pairs,),
            in_specs=[
                mine,
                whole,
                whole,
                mine,
                mine,
                pl.BlockSpec((1, count, 8, rows), lambda p, at: (p, 0, 0, 0)),
                whole,
                whole,
            ],
            out_specs=[mine, whole],
            scratch_shapes=[
                pltpu.VMEM((2, length, PAIR), bf16),
                pltpu.VMEM((2, PAIR, length), bf16),
                pltpu.VMEM((2, length, PAIR), bf16),
                pltpu.VMEM((length, PAIR), f32),
                pltpu.VMEM((length, PAIR), f32),
            ],
        ),
        out_shape=[
            jax.ShapeDtypeStruct(queries.shape, bf16),
            jax.ShapeDtypeStruct((count, rows, PAIR), bf16),
        ],
        compiler_params=pltpu.CompilerParams(vmem_limit_bytes=32 * MIB),
        cost_estimate=pl.CostEstimate(flops=1, bytes_accessed=1, transcendentals=0),
        name="attend_back",
    )(place, queries, keys, values, attended, back, logsum, cosine, sine)


def take_columns_kernel(shards, count, piece, place_ref, gate_ref, up_ref, out_ref):
    width = shards * piece
    for c in range(count):

        @pl.when(place_ref[0] == c)
        def _(c=c):
            for at, ref in ((0, gate_ref), (width, up_ref)):
                pieces = []
                for s in range(shards):
                    start = (s * count + c) * piece
                    pieces.append(ref[:, start : start + piece].astype(f32))
                out_ref[:, at : at + width] = jnp.concatenate(pieces, axis=1).astype(bf16)


def take_columns(place, w_gate, w_up, shards, count):
    rows, ff = w_gate.shape
    piece = ff // (shards * count)
    step = min(rows, 128)
    block = lambda last: pl.BlockSpec((step, last), lambda i, at: (i, 0))
    return pl.pallas_call(
        functools.partial(take_columns_kernel, shards, count, piece),
        grid_spec=pltpu.PrefetchScalarGridSpec(
            num_scalar_prefetch=1,
            grid=(rows // step,),
            in_specs=[block(ff), block(ff)],
            out_specs=block(2 * shards * piece),
        ),
        out_shape=jax.ShapeDtypeStruct((rows, 2 * shards * piece), bf16),
        compiler_params=pltpu.CompilerParams(vmem_limit_bytes=32 * MIB),
        cost_estimate=pl.CostEstimate(flops=1, bytes_accessed=1, transcendentals=0),
        name="take_columns",
    )(place, w_gate, w_up)


def read_blocks(place, refs, sorted_s):
    count = sorted_s.shape[0]
    for r in range(min(count, len(refs))):
        if r == count - 1 and len(refs) > count:
            first = 2 * pl.program_id(0) < pl.num_programs(0)

            @pl.when(first)
            def _():
                sorted_s[place ^ r] = refs[r][...]

            @pl.when(jnp.logical_not(first))
            def _():
                sorted_s[place ^ r] = refs[r + 1][...]
        else:
            sorted_s[place ^ r] = refs[r][...]
    return [sorted_s[a].astype(f32) for a in range(count)]


def block_specs(step, blocks, far):
    wide = blocks[0].shape[1]
    half = max(1, blocks[0].shape[0] // 2 // step)
    return [pl.BlockSpec((step, wide), lambda i, at: (i, 0))] * len(blocks) + [
        pl.BlockSpec((step, wide), lambda i, at: (i % half, 0))
    ] * len(far)


def put_columns_kernel(shards, count, piece, given, place_ref, *refs):
    gate_w, up_w, gain_ref, gate_ref, up_ref, gain_out = refs[given:-1]
    width = shards * piece
    blocks = read_blocks(place_ref[0], refs[:given], refs[-1])
    total = None
    for at, weight, out in ((0, gate_w, gate_ref), (width, up_w, up_ref)):
        for s in range(shards):
            pieces = [one[:, at + s * piece : at + (s + 1) * piece] for one in blocks]
            joined = jnp.concatenate(pieces, axis=1)
            here = slice(s * count * piece, (s + 1) * count * piece)
            out[:, here] = joined
        term = jnp.sum(out[...] * weight[...].astype(f32), axis=1, keepdims=True)
        total = term if total is None else total + term
    gain_out[...] = jnp.broadcast_to(total, (total.shape[0], 128)).T[:1] / gain_ref[...].astype(f32)


def put_columns(place, blocks, far, w_gate, w_up, gain, shards):
    count = len(blocks) + (1 if far else 0)
    given = len(blocks) + len(far)
    rows, ff = w_gate.shape
    piece = ff // (shards * count)
    step = min(rows, 128)
    block = lambda last: pl.BlockSpec((step, last), lambda i, at: (i, 0))
    flat = pl.BlockSpec((1, step), lambda i, at: (0, i))
    return pl.pallas_call(
        functools.partial(put_columns_kernel, shards, count, piece, given),
        grid_spec=pltpu.PrefetchScalarGridSpec(
            num_scalar_prefetch=1,
            grid=(rows // step,),
            in_specs=block_specs(step, blocks, far) + [block(ff), block(ff), flat],
            out_specs=[block(ff), block(ff), flat],
            scratch_shapes=[pltpu.VMEM((count, step, blocks[0].shape[1]), bf16)],
        ),
        out_shape=[
            jax.ShapeDtypeStruct((rows, ff), f32),
            jax.ShapeDtypeStruct((rows, ff), f32),
            jax.ShapeDtypeStruct((1, rows), f32),
        ],
        compiler_params=pltpu.CompilerParams(vmem_limit_bytes=58 * MIB),
        cost_estimate=pl.CostEstimate(flops=1, bytes_accessed=1, transcendentals=0),
        name="put_columns",
    )(place, *blocks, *far, w_gate, w_up, gain)


def put_attention_kernel(count, copies, width_q, given, place_ref, *refs):
    q_w, k_w, v_w, gain_ref, q_ref, k_ref, v_ref, o_ref, gain_out = refs[given:-1]
    blocks = read_blocks(place_ref[0], refs[:given], refs[-1])
    width_o = o_ref.shape[1] // count
    for a in range(count):
        q_ref[:, a * width_q : (a + 1) * width_q] = blocks[a][:, :width_q]
        o_ref[:, a * width_o : (a + 1) * width_o] = blocks[a][:, width_q + PAIR :]
    for part, out in ((0, k_ref), (HEAD_DIM, v_ref)):
        heads = []
        for h in range(count // copies):
            one = None
            for c in range(copies):
                at = width_q + part
                term = blocks[h * copies + c][:, at : at + HEAD_DIM]
                one = term if one is None else one + term
            heads.append(one)
        out[...] = jnp.concatenate(heads, axis=1)
    total = None
    for weight, out in ((q_w, q_ref), (k_w, k_ref), (v_w, v_ref)):
        term = jnp.sum(out[...] * weight[...].astype(f32), axis=1, keepdims=True)
        total = term if total is None else total + term
    gain_out[...] = jnp.broadcast_to(total, (total.shape[0], 128)).T[:1] / gain_ref[...].astype(f32)


def put_attention(place, blocks, far, w_query, w_key, w_value, gain, width, copies):
    count = len(blocks) + (1 if far else 0)
    given = len(blocks) + len(far)
    rows, wide_q = w_query.shape
    wide_k = w_key.shape[1]
    step = min(rows, 128)
    block = lambda last: pl.BlockSpec((step, last), lambda i, at: (i, 0))
    flat = pl.BlockSpec((1, step), lambda i, at: (0, i))
    return pl.pallas_call(
        functools.partial(put_attention_kernel, count, copies, wide_q // count, given),
        grid_spec=pltpu.PrefetchScalarGridSpec(
            num_scalar_prefetch=1,
            grid=(rows // step,),
            in_specs=block_specs(step, blocks, far)
            + [block(wide_q), block(wide_k), block(wide_k), flat],
            out_specs=[block(wide_q), block(wide_k), block(wide_k), block(width), flat],
            scratch_shapes=[pltpu.VMEM((count, step, blocks[0].shape[1]), bf16)],
        ),
        out_shape=[
            jax.ShapeDtypeStruct((rows, last), f32) for last in (wide_q, wide_k, wide_k, width)
        ]
        + [jax.ShapeDtypeStruct((1, rows), f32)],
        compiler_params=pltpu.CompilerParams(vmem_limit_bytes=32 * MIB),
        cost_estimate=pl.CostEstimate(flops=1, bytes_accessed=1, transcendentals=0),
        name="put_attention",
    )(place, *blocks, *far, w_query, w_key, w_value, gain)


def on_device(
    tokens, w_query, w_key, w_value, w_out, w_gate, w_up, w_down, gain_attn, gain_mlp, cotangent
):
    count = lax.axis_size("seq")
    shards = lax.axis_size("shard")
    place = lax.axis_index("seq")
    mine = tokens[0]
    rows, width = mine.shape
    length = rows * count
    width_q = HEADS * HEAD_DIM // count
    local_kv = max(1, KV_HEADS // count)
    copies = count * local_kv // KV_HEADS
    width_kv = local_kv * HEAD_DIM
    assert width_kv == HEAD_DIM
    ff = w_gate.shape[1]
    piece = ff // (shards * count)
    width_f = shards * piece
    place_arg = place.reshape(1).astype(jnp.int32)

    def columns(weight, start, size):
        return lax.dynamic_slice_in_dim(weight, start, size, axis=1)

    def from_shards(block):
        return lax.all_gather(block, "shard", axis=0, tiled=True)

    kv_start = (place * local_kv // copies) * HEAD_DIM
    part_d = width // count
    width_qkv = width_q + PAIR
    gains = lax.all_gather(jnp.stack([gain_attn, gain_mlp]), "shard", axis=1, tiled=True)
    gain_first, gain_second = gains[0:1], gains[1:2].astype(f32)
    w_attn = from_shards(
        jnp.concatenate(
            [
                columns(w_query, place * width_q, width_q),
                columns(w_key, kv_start, width_kv),
                columns(w_value, kv_start, width_kv),
                columns(w_out, place * part_d, part_d),
            ],
            axis=1,
        )
    )
    input_near = gather_near(mine)
    input_near, (gate_in, up_in) = tie(input_near, (w_gate, w_up))
    input_blocks, input_far = gather_far(mine, input_near)
    w_gu = from_shards(take_columns(place_arg, gate_in, up_in, shards, count))
    w_dn = from_shards(lax.dynamic_slice_in_dim(w_down, place * piece, piece, axis=0))

    blocks_at = place ^ jnp.arange(count)
    positions = (blocks_at[:, None] * rows + jnp.arange(rows)[None, :]).astype(f32)
    half_dim = HEAD_DIM // 2
    lanes = jnp.arange(PAIR)
    frequency = jnp.exp(-math.log(THETA) * (lanes % half_dim).astype(f32) * 2.0 / HEAD_DIM)
    angles = positions[:, :, None] * frequency
    cosine = jnp.cos(angles)
    sine = jnp.sin(angles) * jnp.where(lanes % HEAD_DIM < half_dim, -1.0, 1.0)

    normed, queries, keys, values = project(
        [*input_blocks, *input_far], gain_first, w_attn, cosine, sine, width_q
    )
    w_attn, queries = tie(w_attn, queries)

    w_o = jnp.zeros((width_q, width), bf16)
    for r in range(count):
        rows_r = lax.dynamic_slice(
            w_attn, ((place ^ r) * width_q, width_qkv), (width_q, part_d)
        )
        rows_r = hop(rows_r, r) if r else rows_r
        w_o = lax.dynamic_update_slice_in_dim(w_o, rows_r, (place ^ r) * part_d, axis=1)

    attended, attended_t, logsum = attend(place_arg, queries, keys, values)
    attended_rows = attended.reshape(length, width_q)

    def split(array):
        array = array.astype(bf16)
        return [array[r * rows : (r + 1) * rows] for r in range(count)]

    def token_sum(left, right):
        return jnp.einsum("tf,td->fd", left, right, preferred_element_type=f32).astype(bf16)

    def to_owners(part):
        return lax.psum_scatter(part, "shard", scatter_dimension=0, tiled=True)

    parts = split(jnp.dot(attended_rows, w_o, preferred_element_type=f32))
    kept, arrived = scatter_pieces(scatter_turn(scatter_start(parts)))
    middle, upper, lower = norm(kept, arrived, mine, gains[1:2])
    normed_mlp = jnp.concatenate(gather_halves(upper, lower), axis=0)
    normed_mlp, cot = tie(normed_mlp, cotangent[0])
    cot_near = gather_near(cot)
    gate_up = jnp.dot(normed_mlp, w_gu, preferred_element_type=f32)
    gate_up, cot_near = tie(gate_up, cot_near)
    cot_blocks, cot_far = gather_far(cot, cot_near)
    back_mlp = jnp.concatenate([*cot_blocks, *cot_far], axis=0)
    gate_lin, upward = gate_up[:, :width_f], gate_up[:, width_f:]
    sigmoid_gate = jax.nn.sigmoid(gate_lin)
    silu_gate = gate_lin * sigmoid_gate
    hidden = (silu_gate * upward).astype(bf16)
    down_part = token_sum(hidden, back_mlp)

    w_dn, down_part = tie(w_dn, down_part)
    own_down = to_owners(down_part)
    out_parts = split(jnp.dot(hidden, w_dn, preferred_element_type=f32))
    w_dn, out_parts = tie(w_dn, out_parts)
    kept, turning, straight = scatter_start(out_parts)
    back_hidden = (
        jnp.einsum("td,fd->tf", back_mlp, w_dn, preferred_element_type=f32).astype(bf16).astype(f32)
    )
    back_gate = back_hidden * upward * sigmoid_gate * (1.0 + gate_lin * (1.0 - sigmoid_gate))
    back_up = back_hidden * silu_gate
    back_gu = jnp.concatenate([back_gate.astype(bf16), back_up.astype(bf16)], axis=1)

    turning, back_gu = tie(turning, back_gu)
    kept, sent, straight = scatter_turn((kept, turning, straight))

    parts = split(jnp.einsum("tf,df->td", back_gu, w_gu, preferred_element_type=f32))
    parts, (sent, straight) = tie(parts, (sent, straight))
    output = (middle + scatter_end((kept, sent, straight))).astype(bf16)[None]
    parts, turning, straight = scatter_start(parts)
    gu_part = token_sum(normed_mlp, back_gu)
    (turning, straight), gu_part = tie((turning, straight), gu_part)
    state = scatter_turn((parts, turning, straight))
    own_gu = to_owners(gu_part)
    kept, arrived = scatter_pieces(state)

    back_middle, upper, lower = norm_back(kept, arrived, middle, cot, gains[1:2], True)
    pieces, own_down = tie(gather_halves(upper, lower), own_down)
    back_attended, *out_blocks = branch(place_arg, pieces, w_o, attended_t)
    out_blocks = [hop(one, r) if r else one for r, one in enumerate(out_blocks)]
    down_near = gather_near(own_down)
    back_query, back_kv = attend_back(
        place_arg, queries, keys, values, attended, back_attended, logsum, cosine, sine
    )
    back_query, (out_blocks, down_near) = tie(back_query, (out_blocks, down_near))
    back_query, back_kv = back_query.reshape(length, -1), back_kv.reshape(length, -1)
    parts = input_grads(back_query, back_kv, w_attn)
    down_blocks, down_far = gather_far(own_down, down_near)
    if count == 4:
        turning = (hop(parts[3], 1), hop(parts[4], 2))
        parts, back_query = tie(parts, back_query)
    attn_part = attention_grads(
        place_arg, normed.reshape(length, width), back_query, back_kv, out_blocks
    )
    if count == 4:
        (turning, down_far), attn_part = tie((turning, down_far), attn_part)
    attn_part, own_gu = tie(attn_part, own_gu)
    own_attn = to_owners(attn_part)
    gu_near = gather_near(own_gu)
    if count == 4:
        to_near = turn(parts[1:3], turning)
        to_near, gu_near = tie(to_near, gu_near)
        kept, arrived = parts[0], (hop(to_near[0], 1), hop(to_near[1], 2))
    else:
        kept, arrived = scatter_pieces(scatter_turn(scatter_start(parts)))
    gu_blocks, gu_far = gather_far(own_gu, gu_near)
    arrived, own_attn = tie(arrived, own_attn)
    attn_blocks = [own_attn] + [hop(own_attn, r) for r in range(1, count)]
    (grad_tokens,) = norm_back(kept, arrived, mine, back_middle, gain_first, False)
    gu_far, grad_tokens = tie(gu_far, grad_tokens)

    grad_down = jnp.zeros((count * piece, width), f32)
    places = [((place ^ r) * piece, block) for r, block in enumerate(down_blocks)]
    for at, block in enumerate(down_far):
        places.append(((place ^ (count - 1)) * piece + at * (piece // 2), block))
    for at, block in places:
        grad_down = lax.dynamic_update_slice_in_dim(grad_down, block.astype(f32), at, axis=0)
    grad_gate, grad_up, grad_gain_mlp = put_columns(
        place_arg,
        gu_blocks,
        gu_far,
        w_gate,
        w_up,
        gain_mlp.reshape(1, -1),
        shards,
    )
    attn_blocks, (grad_gate, grad_up) = tie(attn_blocks, (grad_gate, grad_up))
    grad_query, grad_key, grad_value, grad_out, grad_gain_attn = put_attention(
        place_arg,
        attn_blocks,
        (),
        w_query,
        w_key,
        w_value,
        gain_attn.reshape(1, -1),
        width,
        copies,
    )
    return (
        output,
        grad_tokens[None],
        grad_query,
        grad_key,
        grad_value,
        grad_out,
        grad_gate,
        grad_up,
        grad_down,
        grad_gain_attn.reshape(-1),
        grad_gain_mlp.reshape(-1),
    )


def solution(mesh):
    rows = P("shard", "seq", None)
    weight = P("shard", None)
    gain = P("shard")
    in_specs = (rows,) + (weight,) * 7 + (gain, gain, rows)
    out_specs = (rows, rows) + (weight,) * 7 + (gain, gain)
    return jax.shard_map(
        on_device, mesh=mesh, in_specs=in_specs, out_specs=out_specs, check_vma=False
    )
```

```python
import functools
import math

import jax
import jax.numpy as jnp
from jax import lax
from jax.experimental import pallas as pl
from jax.experimental.pallas import tpu as pltpu
from jax.sharding import PartitionSpec as P

HEADS = 32
KV_HEADS = 4
HEAD_DIM = 64
PAIR = 2 * HEAD_DIM

EPSILON = 1e-05
THETA = 10000.0
MASKED = -1e30
MIB = 2**20

f32 = jnp.float32
bf16 = jnp.bfloat16

NT = (((1,), (1,)), ((), ()))


def hop(value, bit):
    count = lax.axis_size("seq")
    return lax.ppermute(value, "seq", [(i, i ^ bit) for i in range(count)])


def tie(first, second):
    return lax.optimization_barrier((first, second))


def gather_seq(block, filler=None):
    count = lax.axis_size("seq")
    pieces = block if isinstance(block, tuple) else None
    if pieces is not None:
        block = jnp.concatenate(pieces, axis=0)
    blocks = [block]
    if count == 2:
        blocks.append(hop(block, 1))
    if count >= 4:
        half = block.shape[0] // 2
        upper, lower = pieces or (block[:half], block[half:])
        near_upper, other_lower = hop(upper, 1), hop(lower, 2)
        near_lower, other_upper = hop(lower, 1), hop(upper, 2)
        if filler is not None:
            (near_upper, other_lower), filler = tie((near_upper, other_lower), filler)
        far_upper, far_lower = hop(near_upper, 2), hop(other_lower, 1)
        blocks.append(jnp.concatenate([near_upper, near_lower], axis=0))
        blocks.append(jnp.concatenate([other_upper, other_lower], axis=0))
        blocks.append(jnp.concatenate([far_upper, far_lower], axis=0))
    bit = 4
    while bit < count:
        blocks += [hop(one, bit) for one in blocks]
        bit *= 2
    return blocks if filler is None else (blocks, filler)


def gather_halves(upper, lower):
    if lax.axis_size("seq") != 4:
        return gather_seq(jnp.concatenate([upper, lower], axis=0))
    near_upper, other_lower = hop(upper, 1), hop(lower, 2)
    near_lower, other_upper = hop(lower, 1), hop(upper, 2)
    far_upper, far_lower = hop(near_upper, 2), hop(other_lower, 1)
    return [upper, lower, near_upper, near_lower, other_upper, other_lower, far_upper, far_lower]


def gather_near(block):
    return (hop(block, 1), hop(block, 2)) if lax.axis_size("seq") == 4 else ()


def gather_far(block, near):
    if not near:
        return gather_seq(block), ()
    half = block.shape[0] // 2
    return [block, *near], (hop(near[0][:half], 2), hop(near[1][half:], 1))


def add_low(first, second):
    return (first.astype(f32) + second.astype(f32)).astype(bf16)


def scatter_start(parts):
    count = lax.axis_size("seq")
    bit = count // 2
    while bit >= 4:
        there = [hop(parts[bit + r], bit) for r in range(bit)]
        parts = [add_low(parts[r], there[r]) for r in range(bit)]
        bit //= 2
    if count < 4:
        return parts, (), tuple(hop(one, 1) for one in parts[1:])
    half = parts[3].shape[0] // 2
    turning = (hop(parts[3][:half], 1), hop(parts[3][half:], 2))
    straight = (hop(parts[1][:half], 1), hop(parts[2][half:], 2))
    return parts, turning, straight


def scatter_turn(state):
    parts, turning, straight = state
    if not turning:
        return parts[0], (), straight
    half = parts[3].shape[0] // 2
    sent_y = hop(add_low(parts[2][:half], turning[0]), 2)
    sent_x = hop(add_low(parts[1][half:], turning[1]), 1)
    return parts[0], (sent_x, sent_y), straight


def scatter_pieces(state):
    kept, sent, straight = state
    if not sent:
        return scatter_end(state), ()
    return kept, (straight[0], sent[0], sent[1], straight[1])


def scatter_end(state):
    kept, sent, straight = state
    total = kept.astype(f32)
    if not sent:
        for one in straight:
            total = total + one.astype(f32)
        return total
    total = total + jnp.concatenate([straight[0], sent[0]], axis=0).astype(f32)
    return total + jnp.concatenate([sent[1], straight[1]], axis=0).astype(f32)


def scatter_seq(parts):
    return scatter_end(scatter_turn(scatter_start(parts)))


def rms_scale(values):
    return lax.rsqrt(jnp.mean(values * values, axis=-1, keepdims=True) + EPSILON)


def lane_in_first_half(shape):
    return lax.broadcasted_iota(jnp.int32, shape, 1) < HEAD_DIM


def swap_quarters(values):
    quarter = HEAD_DIM // 2
    lane = lax.broadcasted_iota(jnp.int32, values.shape, 1)
    return jnp.where(
        lane % HEAD_DIM < quarter,
        pltpu.roll(values, PAIR - quarter, 1),
        pltpu.roll(values, quarter, 1),
    )


def branch_kernel(count, given, place_ref, w_ref, t_ref, *refs):
    back_ref, out_refs, rows_s = refs[given], refs[given + 1 : -1], refs[-1]
    step = pl.program_id(0)

    @pl.when(step == 0)
    def _():
        at = 0
        for ref in refs[:given]:
            rows_s[at : at + ref.shape[0], :] = ref[...]
            at += ref.shape[0]

    rows = rows_s.shape[0] // count
    part = rows_s.shape[1] // count
    block = rows_s[pl.ds(pl.multiple_of(step * rows, rows), rows), :]
    back_ref[0] = lax.dot_general(
        block, w_ref[...], NT, preferred_element_type=f32
    ).astype(bf16)
    columns = rows_s[:, pl.ds(pl.multiple_of(step * part, part), part)]
    result = jnp.dot(t_ref[...], columns, preferred_element_type=f32).astype(bf16)
    for r in range(count):

        @pl.when(step == place_ref[0] ^ r)
        def _(r=r):
            out_refs[r][...] = result


def branch(place, pieces, w_o, attended_t):
    count = lax.axis_size("seq")
    width_q, length = attended_t.shape
    width = w_o.shape[1]
    rows, part = length // count, width // count
    whole = lambda shape: pl.BlockSpec(shape, lambda i, at: (0,) * len(shape))
    return pl.pallas_call(
        functools.partial(branch_kernel, count, len(pieces)),
        grid_spec=pltpu.PrefetchScalarGridSpec(
            num_scalar_prefetch=1,
            grid=(count,),
            in_specs=[whole(w_o.shape), whole(attended_t.shape)]
            + [whole(one.shape) for one in pieces],
            out_specs=[pl.BlockSpec((1, rows, width_q), lambda i, at: (i, 0, 0))]
            + [whole((width_q, part))] * count,
            scratch_shapes=[pltpu.VMEM((length, width), bf16)],
        ),
        out_shape=[jax.ShapeDtypeStruct((count, rows, width_q), bf16)]
        + [jax.ShapeDtypeStruct((width_q, part), bf16)] * count,
        compiler_params=pltpu.CompilerParams(vmem_limit_bytes=60 * MIB),
        cost_estimate=pl.CostEstimate(flops=1, bytes_accessed=1, transcendentals=0),
        name="branch",
    )(place, w_o, attended_t, *pieces)


def attention_grads_kernel(count, place_ref, n_ref, dq_ref, dkv_ref, *refs):
    out_refs, part_ref, sorted_s = refs[:count], refs[count], refs[count + 1]

    @pl.when(pl.program_id(0) == 0)
    def _():
        for r in range(count):
            sorted_s[place_ref[0] ^ r] = out_refs[r][...]

    def token_sum(left, right):
        return lax.dot_general(
            left, right, (((0,), (0,)), ((), ())), preferred_element_type=f32
        ).astype(bf16)

    width_q = dq_ref.shape[1]
    normed = n_ref[...]
    part_ref[:, :width_q] = token_sum(normed, dq_ref[...])
    part_ref[:, width_q : width_q + PAIR] = token_sum(normed, dkv_ref[...])
    part_ref[:, width_q + PAIR :] = sorted_s[pl.program_id(0)]


def attention_grads(place, normed, back_query, back_kv, out_blocks):
    count = len(out_blocks)
    length, width = normed.shape
    width_q = back_query.shape[1]
    part_q, part_d = out_blocks[0].shape
    whole = lambda shape: pl.BlockSpec(shape, lambda a, at: (0, 0))
    wide = width_q + PAIR + part_d
    return pl.pallas_call(
        functools.partial(attention_grads_kernel, count),
        grid_spec=pltpu.PrefetchScalarGridSpec(
            num_scalar_prefetch=1,
            grid=(count,),
            in_specs=[
                pl.BlockSpec((length, part_q), lambda a, at: (0, a)),
                whole((length, width_q)),
                whole((length, PAIR)),
            ]
            + [whole((part_q, part_d))] * count,
            out_specs=pl.BlockSpec((part_q, wide), lambda a, at: (a, 0)),
            scratch_shapes=[pltpu.VMEM((count, part_q, part_d), bf16)],
        ),
        out_shape=jax.ShapeDtypeStruct((width, wide), bf16),
        compiler_params=pltpu.CompilerParams(vmem_limit_bytes=60 * MIB),
        cost_estimate=pl.CostEstimate(flops=1, bytes_accessed=1, transcendentals=0),
        name="attention_grads",
    )(place, normed, back_query, back_kv, *out_blocks)


def input_grads_kernel(count, dq_ref, dkv_ref, w_ref, *outs):
    width_q = dq_ref.shape[1]
    weights = w_ref[...]
    result = lax.dot_general(
        dq_ref[...], weights[:, :width_q], NT, preferred_element_type=f32
    ) + lax.dot_general(dkv_ref[...], weights[:, width_q:], NT, preferred_element_type=f32)
    at = 0
    for out in outs:
        out[...] = result[at : at + out.shape[0], :].astype(bf16)
        at += out.shape[0]


def input_grads(back_query, back_kv, weights):
    count = lax.axis_size("seq")
    length, width_q = back_query.shape
    width = weights.shape[0]
    rows = length // count
    sizes = [rows] * (count - 1) + ([rows // 2] * 2 if count == 4 else [rows])
    step = 512
    whole = lambda shape: pl.BlockSpec(shape, lambda i: (0, 0))
    return pl.pallas_call(
        functools.partial(input_grads_kernel, count),
        grid=(width // step,),
        in_specs=[
            whole(back_query.shape),
            whole(back_kv.shape),
            pl.BlockSpec((step, width_q + PAIR), lambda i: (i, 0)),
        ],
        out_specs=[pl.BlockSpec((size, step), lambda i: (0, i)) for size in sizes],
        out_shape=[jax.ShapeDtypeStruct((size, width), bf16) for size in sizes],
        compiler_params=pltpu.CompilerParams(vmem_limit_bytes=60 * MIB),
        cost_estimate=pl.CostEstimate(flops=1, bytes_accessed=1, transcendentals=0),
        name="input_grads",
    )(back_query, back_kv, weights)


def turn_kernel(x_ref, y_ref, upper_ref, lower_ref, to_x_ref, to_y_ref):
    first = pl.program_id(0) == 0
    to_x, to_y = x_ref[...].astype(f32), y_ref[...].astype(f32)
    to_x_ref[...] = jnp.where(first, to_x, to_x + lower_ref[...].astype(f32)).astype(bf16)
    to_y_ref[...] = jnp.where(first, to_y + upper_ref[...].astype(f32), to_y).astype(bf16)


def turn(parts, turning):
    half, width = turning[0].shape
    part = pl.BlockSpec((half, width), lambda i: (i, 0))
    fixed = pl.BlockSpec((half, width), lambda i: (0, 0))
    return pl.pallas_call(
        turn_kernel,
        grid=(2,),
        in_specs=[part, part, fixed, fixed],
        out_specs=[part, part],
        out_shape=[jax.ShapeDtypeStruct((2 * half, width), bf16)] * 2,
        compiler_params=pltpu.CompilerParams(vmem_limit_bytes=60 * MIB),
        cost_estimate=pl.CostEstimate(flops=1, bytes_accessed=1, transcendentals=0),
        name="turn",
    )(*parts, *turning)


def norm_kernel(given, kept, add_ref, gain_ref, *refs):
    arrived, (middle_ref, upper_ref, lower_ref) = refs[:given], refs[given:]
    first = 2 * pl.program_id(0) < pl.num_programs(0)
    values = kept[...].astype(f32) + add_ref[...].astype(f32)
    if given == 4:
        for upper, lower in (arrived[:2], arrived[2:]):
            values += jnp.where(first, upper[...].astype(f32), lower[...].astype(f32))
    middle_ref[...] = values
    scale = lax.rsqrt(jnp.mean(values * values, axis=-1, keepdims=True) + EPSILON)
    result = (values * scale * gain_ref[...].astype(f32)).astype(bf16)

    @pl.when(first)
    def _():
        upper_ref[...] = result

    @pl.when(jnp.logical_not(first))
    def _():
        lower_ref[...] = result


def norm(kept, arrived, add, gain):
    rows, width = add.shape
    half = rows // 2
    step = half // 2
    block = pl.BlockSpec((step, width), lambda i: (i, 0))
    fixed = pl.BlockSpec((1, width), lambda i: (0, 0))
    upper = pl.BlockSpec((step, width), lambda i: (jnp.minimum(i, 1), 0))
    lower = pl.BlockSpec((step, width), lambda i: (jnp.maximum(i, 2) - 2, 0))
    pieces = [upper, lower] * 2 if len(arrived) == 4 else [block] * len(arrived)
    low = jax.ShapeDtypeStruct((half, width), bf16)
    return pl.pallas_call(
        functools.partial(norm_kernel, len(arrived)),
        grid=(4,),
        in_specs=[block, block, fixed] + pieces,
        out_specs=[block, upper, lower],
        out_shape=[jax.ShapeDtypeStruct((rows, width), f32), low, low],
        compiler_params=pltpu.CompilerParams(vmem_limit_bytes=60 * MIB),
        cost_estimate=pl.CostEstimate(flops=1, bytes_accessed=1, transcendentals=0),
        name="norm",
    )(kept, add, gain, *arrived)


def norm_back_kernel(given, *refs):
    kept, values_ref, add_ref, gain_ref = refs[:4]
    arrived, outs = refs[4 : 4 + given], refs[4 + given :]
    back = kept[...].astype(f32)
    first = 2 * pl.program_id(0) < pl.num_programs(0)
    if given == 2:
        back += arrived[0][...].astype(f32) + arrived[1][...].astype(f32)
    if given == 4:
        for upper, lower in (arrived[:2], arrived[2:]):
            back += jnp.where(first, upper[...].astype(f32), lower[...].astype(f32))
    values = values_ref[...].astype(f32)
    branch = back * gain_ref[...].astype(f32)
    scale = lax.rsqrt(jnp.mean(values * values, axis=-1, keepdims=True) + EPSILON)
    inner = jnp.mean(branch * values, axis=-1, keepdims=True)
    result = add_ref[...].astype(f32) + scale * (branch - values * (scale * scale * inner))
    outs[0][...] = result
    if len(outs) == 3:

        @pl.when(first)
        def _():
            outs[1][...] = result.astype(bf16)

        @pl.when(jnp.logical_not(first))
        def _():
            outs[2][...] = result.astype(bf16)


def norm_back(kept, arrived, values, add, gain, halves):
    rows, width = values.shape
    half = rows // 2
    step = half // 2
    block = pl.BlockSpec((step, width), lambda i: (i, 0))
    fixed = pl.BlockSpec((1, width), lambda i: (0, 0))
    upper = pl.BlockSpec((step, width), lambda i: (jnp.minimum(i, 1), 0))
    lower = pl.BlockSpec((step, width), lambda i: (jnp.maximum(i, 2) - 2, 0))
    pieces = [upper, lower] * 2 if len(arrived) == 4 else [block] * len(arrived)
    low = jax.ShapeDtypeStruct((half, width), bf16)
    return pl.pallas_call(
        functools.partial(norm_back_kernel, len(arrived)),
        grid=(4,),
        in_specs=[block, block, block, fixed] + pieces,
        out_specs=[block] + ([upper, lower] if halves else []),
        out_shape=[jax.ShapeDtypeStruct((rows, width), f32)] + [low] * (2 if halves else 0),
        compiler_params=pltpu.CompilerParams(vmem_limit_bytes=60 * MIB),
        cost_estimate=pl.CostEstimate(flops=1, bytes_accessed=1, transcendentals=0),
        name="norm_back",
    )(kept, values, add, gain, *arrived)


def spread_blocks(count, refs, store):
    for r in range(count):
        if r == count - 1 and len(refs) > count:
            store(r, 0, refs[r])
            store(r, refs[r].shape[0], refs[r + 1])
        else:
            store(r, 0, refs[r])


def project_kernel(count, width_q, given, *refs):
    gain_ref, w_ref, cos_ref, sin_ref, n_ref, q_ref, k_ref, v_ref, x_s = refs[given:]

    def store(r, at, ref):
        @pl.when(pl.program_id(0) == r)
        def _():
            x_s[at : at + ref.shape[0], :] = ref[...]

    spread_blocks(count, refs[:given], store)
    values = x_s[...].astype(f32)
    scale = lax.rsqrt(jnp.mean(values * values, axis=-1, keepdims=True) + EPSILON)
    normed = (values * scale * gain_ref[...].astype(f32)).astype(bf16)
    n_ref[0] = normed
    lin = jnp.dot(normed, w_ref[...], preferred_element_type=f32)
    cosine, sine = cos_ref[0], sin_ref[0]
    for at in range(0, width_q, PAIR):
        part = lin[:, at : at + PAIR]
        turned = (part * cosine + swap_quarters(part) * sine).astype(bf16)
        q_ref[0, :, at : at + PAIR] = (turned.astype(f32) * HEAD_DIM**-0.5).astype(bf16)
    both = lin[:, width_q : width_q + PAIR]
    swapped = pltpu.roll(both, HEAD_DIM, 1)
    first = lane_in_first_half(both.shape)
    keys = jnp.where(first, both, swapped)
    k_ref[0] = (keys * cosine + swap_quarters(keys) * sine).astype(bf16)
    v_ref[0] = jnp.where(first, swapped, both).astype(bf16)


def project(blocks, gain, weights, cosine, sine, width_q):
    count = lax.axis_size("seq")
    rows, width = blocks[0].shape
    row_block = lambda last: pl.BlockSpec((1, rows, last), lambda i: (i, 0, 0))
    whole = lambda shape: pl.BlockSpec(shape, lambda i: (0,) * len(shape))
    shape = lambda last: jax.ShapeDtypeStruct((count, rows, last), bf16)
    return pl.pallas_call(
        functools.partial(project_kernel, count, width_q, len(blocks)),
        grid=(count,),
        in_specs=[whole(one.shape) for one in blocks]
        + [
            whole((1, width)),
            whole((width, width_q + PAIR)),
            row_block(PAIR),
            row_block(PAIR),
        ],
        out_specs=[row_block(width), row_block(width_q), row_block(PAIR), row_block(PAIR)],
        out_shape=[shape(width), shape(width_q), shape(PAIR), shape(PAIR)],
        scratch_shapes=[pltpu.VMEM((rows, width), bf16)],
        compiler_params=pltpu.CompilerParams(vmem_limit_bytes=60 * MIB),
        cost_estimate=pl.CostEstimate(flops=1, bytes_accessed=1, transcendentals=0),
        name="project",
    )(*blocks, gain, weights, cosine, sine)


def take_keys(count, rows, place, k_ref, v_ref, keys_of, values_of):
    for r in range(count):
        at = pl.multiple_of((place ^ r) * rows, rows)
        keys, values = k_ref[r], v_ref[r]
        first = lane_in_first_half(keys.shape)
        zero = jnp.zeros_like(keys)
        keys_of(0, at, jnp.where(first, keys, zero))
        keys_of(1, at, jnp.where(first, zero, keys))
        values_of(0, at, jnp.where(first, values, zero))
        values_of(1, at, jnp.where(first, zero, values))


def attend_kernel(
    count, rows, place_ref, q_ref, k_ref, v_ref, o_ref, t_ref, l_ref, key_s, value_s, score_s
):
    block = pl.program_id(1)

    @pl.when((pl.program_id(0) == 0) & (block == 0))
    def _():
        def keys_of(h, at, value):
            key_s[h, pl.ds(at, rows), :] = value

        def values_of(h, at, value):
            value_s[h, :, pl.ds(at, rows)] = value.astype(f32).T.astype(bf16)

        take_keys(count, rows, place_ref[0], k_ref, v_ref, keys_of, values_of)

    key_at = lax.broadcasted_iota(jnp.int32, (rows, rows), 0)
    query_at = lax.broadcasted_iota(jnp.int32, (rows, rows), 1)
    allowed = key_at <= query_at

    for c in range(count):

        @pl.when(block == c)
        def _(c=c):
            queries = q_ref[0]
            total = None
            for h in range(2):
                highest = None
                for t in range(c + 1):
                    scores = lax.dot_general(
                        key_s[h, t * rows : (t + 1) * rows, :],
                        queries,
                        NT,
                        preferred_element_type=f32,
                    )
                    if t == c:
                        scores = jnp.where(allowed, scores, MASKED)
                    score_s[h, t * rows : (t + 1) * rows, :] = scores
                    top = jnp.max(scores, axis=0, keepdims=True)
                    highest = top if highest is None else jnp.maximum(highest, top)
                weight = None
                result = None
                for t in range(c + 1):
                    exponent = jnp.exp(score_s[h, t * rows : (t + 1) * rows, :] - highest)
                    one = jnp.sum(exponent, axis=0, keepdims=True)
                    weight = one if weight is None else weight + one
                    part = jnp.dot(
                        value_s[h, :, t * rows : (t + 1) * rows],
                        exponent.astype(bf16),
                        preferred_element_type=f32,
                    )
                    result = part if result is None else result + part
                l_ref[0, 0, h : h + 1, :] = highest + jnp.log(weight)
                result = result / weight
                total = result if total is None else total + result
            o_ref[0] = total.T.astype(bf16)
            t_ref[...] = total.astype(bf16)


def attend(place, queries, keys, values):
    count, rows, width = queries.shape
    pairs = width // PAIR
    length = count * rows
    whole = pl.BlockSpec((count, rows, PAIR), lambda p, i, at: (0, 0, 0))
    mine = pl.BlockSpec((1, rows, PAIR), lambda p, i, at: (i ^ at[0], 0, p))
    return pl.pallas_call(
        functools.partial(attend_kernel, count, rows),
        grid_spec=pltpu.PrefetchScalarGridSpec(
            num_scalar_prefetch=1,
            grid=(pairs, count),
            in_specs=[mine, whole, whole],
            out_specs=[
                mine,
                pl.BlockSpec((PAIR, rows), lambda p, i, at: (p, i ^ at[0])),
                pl.BlockSpec((1, 1, 8, rows), lambda p, i, at: (p, i, 0, 0)),
            ],
            scratch_shapes=[
                pltpu.VMEM((2, length, PAIR), bf16),
                pltpu.VMEM((2, PAIR, length), bf16),
                pltpu.VMEM((2, length, rows), f32),
            ],
        ),
        out_shape=[
            jax.ShapeDtypeStruct(queries.shape, bf16),
            jax.ShapeDtypeStruct((width, length), bf16),
            jax.ShapeDtypeStruct((pairs, count, 8, rows), f32),
        ],
        compiler_params=pltpu.CompilerParams(vmem_limit_bytes=24 * MIB),
        cost_estimate=pl.CostEstimate(flops=1, bytes_accessed=1, transcendentals=0),
        name="attend",
    )(place, queries, keys, values)


def attend_back_kernel(
    count,
    rows,
    place_ref,
    q_ref,
    k_ref,
    v_ref,
    o_ref,
    d_ref,
    l_ref,
    cos_ref,
    sin_ref,
    dq_ref,
    dkv_ref,
    key_s,
    flat_s,
    value_s,
    dk_s,
    dv_s,
):
    pair = pl.program_id(0)
    place = place_ref[0]

    @pl.when(pair == 0)
    def _():
        def keys_of(h, at, value):
            key_s[h, pl.ds(at, rows), :] = value
            flat_s[h, :, pl.ds(at, rows)] = value.astype(f32).T.astype(bf16)

        def values_of(h, at, value):
            value_s[h, pl.ds(at, rows), :] = value

        take_keys(count, rows, place, k_ref, v_ref, keys_of, values_of)
        dk_s[...] = jnp.zeros_like(dk_s)
        dv_s[...] = jnp.zeros_like(dv_s)

    key_at = lax.broadcasted_iota(jnp.int32, (rows, rows), 0)
    query_at = lax.broadcasted_iota(jnp.int32, (rows, rows), 1)
    allowed = key_at <= query_at

    for c in range(count):
        block = place ^ c
        queries, back = q_ref[block], d_ref[block]
        first = lane_in_first_half(queries.shape)
        zero = jnp.zeros_like(queries)
        terms = (back.astype(f32) * o_ref[block].astype(f32)).T
        total = None
        for h in range(2):
            row_term = jnp.sum(terms[h * HEAD_DIM : (h + 1) * HEAD_DIM, :], axis=0, keepdims=True)
            query_h = jnp.where(first, queries, zero) if h == 0 else jnp.where(first, zero, queries)
            back_h = jnp.where(first, back, zero) if h == 0 else jnp.where(first, zero, back)
            logsum = l_ref[0, c, h : h + 1, :]
            for t in range(c + 1):
                at = slice(t * rows, (t + 1) * rows)
                scores = lax.dot_general(
                    key_s[h, at, :], queries, NT, preferred_element_type=f32
                )
                if t == c:
                    scores = jnp.where(allowed, scores, MASKED)
                probs = jnp.exp(scores - logsum)
                back_probs = lax.dot_general(
                    value_s[h, at, :], back, NT, preferred_element_type=f32
                )
                back_scores = (probs * (back_probs - row_term)).astype(bf16)
                dv_s[at, :] += jnp.dot(probs.astype(bf16), back_h, preferred_element_type=f32)
                dk_s[at, :] += jnp.dot(back_scores, query_h, preferred_element_type=f32)
                part = jnp.dot(flat_s[h, :, at], back_scores, preferred_element_type=f32)
                total = part if total is None else total + part
        turned = (total.T * HEAD_DIM**-0.5).astype(bf16).astype(f32)
        dq_ref[block] = (
            turned * cos_ref[block] - swap_quarters(turned) * sin_ref[block]
        ).astype(bf16)

    @pl.when(pair == pl.num_programs(0) - 1)
    def _():
        for r in range(count):
            at = pl.multiple_of((place ^ r) * rows, rows)
            keys = dk_s[pl.ds(at, rows), :]
            values = dv_s[pl.ds(at, rows), :]
            keys = (keys + pltpu.roll(keys, HEAD_DIM, 1)).astype(bf16).astype(f32)
            values = values + pltpu.roll(values, HEAD_DIM, 1)
            keys = keys * cos_ref[r] - swap_quarters(keys) * sin_ref[r]
            dkv_ref[r] = jnp.where(lane_in_first_half(keys.shape), keys, values).astype(bf16)


def attend_back(place, queries, keys, values, attended, back, logsum, cosine, sine):
    count, rows, width = queries.shape
    pairs = width // PAIR
    length = count * rows
    whole = pl.BlockSpec((count, rows, PAIR), lambda p, at: (0, 0, 0))
    mine = pl.BlockSpec((count, rows, PAIR), lambda p, at: (0, 0, p))
    return pl.pallas_call(
        functools.partial(attend_back_kernel, count, rows),
        grid_spec=pltpu.PrefetchScalarGridSpec(
            num_scalar_prefetch=1,
            grid=(pairs,),
            in_specs=[
                mine,
                whole,
                whole,
                mine,
                mine,
                pl.BlockSpec((1, count, 8, rows), lambda p, at: (p, 0, 0, 0)),
                whole,
                whole,
            ],
            out_specs=[mine, whole],
            scratch_shapes=[
                pltpu.VMEM((2, length, PAIR), bf16),
                pltpu.VMEM((2, PAIR, length), bf16),
                pltpu.VMEM((2, length, PAIR), bf16),
                pltpu.VMEM((length, PAIR), f32),
                pltpu.VMEM((length, PAIR), f32),
            ],
        ),
        out_shape=[
            jax.ShapeDtypeStruct(queries.shape, bf16),
            jax.ShapeDtypeStruct((count, rows, PAIR), bf16),
        ],
        compiler_params=pltpu.CompilerParams(vmem_limit_bytes=32 * MIB),
        cost_estimate=pl.CostEstimate(flops=1, bytes_accessed=1, transcendentals=0),
        name="attend_back",
    )(place, queries, keys, values, attended, back, logsum, cosine, sine)


def take_columns_kernel(shards, count, piece, place_ref, gate_ref, up_ref, out_ref):
    width = shards * piece
    for c in range(count):

        @pl.when(place_ref[0] == c)
        def _(c=c):
            for at, ref in ((0, gate_ref), (width, up_ref)):
                pieces = []
                for s in range(shards):
                    start = (s * count + c) * piece
                    pieces.append(ref[:, start : start + piece].astype(f32))
                out_ref[:, at : at + width] = jnp.concatenate(pieces, axis=1).astype(bf16)


def take_columns(place, w_gate, w_up, shards, count):
    rows, ff = w_gate.shape
    piece = ff // (shards * count)
    step = min(rows, 128)
    block = lambda last: pl.BlockSpec((step, last), lambda i, at: (i, 0))
    return pl.pallas_call(
        functools.partial(take_columns_kernel, shards, count, piece),
        grid_spec=pltpu.PrefetchScalarGridSpec(
            num_scalar_prefetch=1,
            grid=(rows // step,),
            in_specs=[block(ff), block(ff)],
            out_specs=block(2 * shards * piece),
        ),
        out_shape=jax.ShapeDtypeStruct((rows, 2 * shards * piece), bf16),
        compiler_params=pltpu.CompilerParams(vmem_limit_bytes=32 * MIB),
        cost_estimate=pl.CostEstimate(flops=1, bytes_accessed=1, transcendentals=0),
        name="take_columns",
    )(place, w_gate, w_up)


def read_blocks(place, refs, sorted_s):
    count = sorted_s.shape[0]
    for r in range(min(count, len(refs))):
        if r == count - 1 and len(refs) > count:
            first = 2 * pl.program_id(0) < pl.num_programs(0)

            @pl.when(first)
            def _():
                sorted_s[place ^ r] = refs[r][...]

            @pl.when(jnp.logical_not(first))
            def _():
                sorted_s[place ^ r] = refs[r + 1][...]
        else:
            sorted_s[place ^ r] = refs[r][...]
    return [sorted_s[a].astype(f32) for a in range(count)]


def block_specs(step, blocks, far):
    wide = blocks[0].shape[1]
    half = max(1, blocks[0].shape[0] // 2 // step)
    return [pl.BlockSpec((step, wide), lambda i, at: (i, 0))] * len(blocks) + [
        pl.BlockSpec((step, wide), lambda i, at: (i % half, 0))
    ] * len(far)


def put_columns_kernel(shards, count, piece, given, place_ref, *refs):
    gate_w, up_w, gain_ref, gate_ref, up_ref, gain_out = refs[given:-1]
    width = shards * piece
    blocks = read_blocks(place_ref[0], refs[:given], refs[-1])
    total = None
    for at, weight, out in ((0, gate_w, gate_ref), (width, up_w, up_ref)):
        for s in range(shards):
            pieces = [one[:, at + s * piece : at + (s + 1) * piece] for one in blocks]
            joined = jnp.concatenate(pieces, axis=1)
            here = slice(s * count * piece, (s + 1) * count * piece)
            out[:, here] = joined
        term = jnp.sum(out[...] * weight[...].astype(f32), axis=1, keepdims=True)
        total = term if total is None else total + term
    gain_out[...] = jnp.broadcast_to(total, (total.shape[0], 128)).T[:1] / gain_ref[...].astype(f32)


def put_columns(place, blocks, far, w_gate, w_up, gain, shards):
    count = len(blocks) + (1 if far else 0)
    given = len(blocks) + len(far)
    rows, ff = w_gate.shape
    piece = ff // (shards * count)
    step = min(rows, 128)
    block = lambda last: pl.BlockSpec((step, last), lambda i, at: (i, 0))
    flat = pl.BlockSpec((1, step), lambda i, at: (0, i))
    return pl.pallas_call(
        functools.partial(put_columns_kernel, shards, count, piece, given),
        grid_spec=pltpu.PrefetchScalarGridSpec(
            num_scalar_prefetch=1,
            grid=(rows // step,),
            in_specs=block_specs(step, blocks, far) + [block(ff), block(ff), flat],
            out_specs=[block(ff), block(ff), flat],
            scratch_shapes=[pltpu.VMEM((count, step, blocks[0].shape[1]), bf16)],
        ),
        out_shape=[
            jax.ShapeDtypeStruct((rows, ff), f32),
            jax.ShapeDtypeStruct((rows, ff), f32),
            jax.ShapeDtypeStruct((1, rows), f32),
        ],
        compiler_params=pltpu.CompilerParams(vmem_limit_bytes=58 * MIB),
        cost_estimate=pl.CostEstimate(flops=1, bytes_accessed=1, transcendentals=0),
        name="put_columns",
    )(place, *blocks, *far, w_gate, w_up, gain)


def put_attention_kernel(count, copies, width_q, given, place_ref, *refs):
    q_w, k_w, v_w, gain_ref, q_ref, k_ref, v_ref, o_ref, gain_out = refs[given:-1]
    blocks = read_blocks(place_ref[0], refs[:given], refs[-1])
    width_o = o_ref.shape[1] // count
    for a in range(count):
        q_ref[:, a * width_q : (a + 1) * width_q] = blocks[a][:, :width_q]
        o_ref[:, a * width_o : (a + 1) * width_o] = blocks[a][:, width_q + PAIR :]
    for part, out in ((0, k_ref), (HEAD_DIM, v_ref)):
        heads = []
        for h in range(count // copies):
            one = None
            for c in range(copies):
                at = width_q + part
                term = blocks[h * copies + c][:, at : at + HEAD_DIM]
                one = term if one is None else one + term
            heads.append(one)
        out[...] = jnp.concatenate(heads, axis=1)
    total = None
    for weight, out in ((q_w, q_ref), (k_w, k_ref), (v_w, v_ref)):
        term = jnp.sum(out[...] * weight[...].astype(f32), axis=1, keepdims=True)
        total = term if total is None else total + term
    gain_out[...] = jnp.broadcast_to(total, (total.shape[0], 128)).T[:1] / gain_ref[...].astype(f32)


def put_attention(place, blocks, far, w_query, w_key, w_value, gain, width, copies):
    count = len(blocks) + (1 if far else 0)
    given = len(blocks) + len(far)
    rows, wide_q = w_query.shape
    wide_k = w_key.shape[1]
    step = min(rows, 128)
    block = lambda last: pl.BlockSpec((step, last), lambda i, at: (i, 0))
    flat = pl.BlockSpec((1, step), lambda i, at: (0, i))
    return pl.pallas_call(
        functools.partial(put_attention_kernel, count, copies, wide_q // count, given),
        grid_spec=pltpu.PrefetchScalarGridSpec(
            num_scalar_prefetch=1,
            grid=(rows // step,),
            in_specs=block_specs(step, blocks, far)
            + [block(wide_q), block(wide_k), block(wide_k), flat],
            out_specs=[block(wide_q), block(wide_k), block(wide_k), block(width), flat],
            scratch_shapes=[pltpu.VMEM((count, step, blocks[0].shape[1]), bf16)],
        ),
        out_shape=[
            jax.ShapeDtypeStruct((rows, last), f32) for last in (wide_q, wide_k, wide_k, width)
        ]
        + [jax.ShapeDtypeStruct((1, rows), f32)],
        compiler_params=pltpu.CompilerParams(vmem_limit_bytes=32 * MIB),
        cost_estimate=pl.CostEstimate(flops=1, bytes_accessed=1, transcendentals=0),
        name="put_attention",
    )(place, *blocks, *far, w_query, w_key, w_value, gain)


def on_device(
    tokens, w_query, w_key, w_value, w_out, w_gate, w_up, w_down, gain_attn, gain_mlp, cotangent
):
    count = lax.axis_size("seq")
    shards = lax.axis_size("shard")
    place = lax.axis_index("seq")
    mine = tokens[0]
    rows, width = mine.shape
    length = rows * count
    width_q = HEADS * HEAD_DIM // count
    local_kv = max(1, KV_HEADS // count)
    copies = count * local_kv // KV_HEADS
    width_kv = local_kv * HEAD_DIM
    assert width_kv == HEAD_DIM
    ff = w_gate.shape[1]
    piece = ff // (shards * count)
    width_f = shards * piece
    place_arg = place.reshape(1).astype(jnp.int32)

    def columns(weight, start, size):
        return lax.dynamic_slice_in_dim(weight, start, size, axis=1)

    def from_shards(block):
        return lax.all_gather(block, "shard", axis=0, tiled=True)

    kv_start = (place * local_kv // copies) * HEAD_DIM
    part_d = width // count
    width_qkv = width_q + PAIR
    gains = lax.all_gather(jnp.stack([gain_attn, gain_mlp]), "shard", axis=1, tiled=True)
    gain_first, gain_second = gains[0:1], gains[1:2].astype(f32)
    w_attn = from_shards(
        jnp.concatenate(
            [
                columns(w_query, place * width_q, width_q),
                columns(w_key, kv_start, width_kv),
                columns(w_value, kv_start, width_kv),
                columns(w_out, place * part_d, part_d),
            ],
            axis=1,
        )
    )
    input_near = gather_near(mine)
    input_near, (gate_in, up_in) = tie(input_near, (w_gate, w_up))
    input_blocks, input_far = gather_far(mine, input_near)
    w_gu = from_shards(take_columns(place_arg, gate_in, up_in, shards, count))
    w_dn = from_shards(lax.dynamic_slice_in_dim(w_down, place * piece, piece, axis=0))

    blocks_at = place ^ jnp.arange(count)
    positions = (blocks_at[:, None] * rows + jnp.arange(rows)[None, :]).astype(f32)
    half_dim = HEAD_DIM // 2
    lanes = jnp.arange(PAIR)
    frequency = jnp.exp(-math.log(THETA) * (lanes % half_dim).astype(f32) * 2.0 / HEAD_DIM)
    angles = positions[:, :, None] * frequency
    cosine = jnp.cos(angles)
    sine = jnp.sin(angles) * jnp.where(lanes % HEAD_DIM < half_dim, -1.0, 1.0)

    normed, queries, keys, values = project(
        [*input_blocks, *input_far], gain_first, w_attn, cosine, sine, width_q
    )
    w_attn, queries = tie(w_attn, queries)

    w_o = jnp.zeros((width_q, width), bf16)
    for r in range(count):
        rows_r = lax.dynamic_slice(
            w_attn, ((place ^ r) * width_q, width_qkv), (width_q, part_d)
        )
        rows_r = hop(rows_r, r) if r else rows_r
        w_o = lax.dynamic_update_slice_in_dim(w_o, rows_r, (place ^ r) * part_d, axis=1)

    attended, attended_t, logsum = attend(place_arg, queries, keys, values)
    attended_rows = attended.reshape(length, width_q)

    def split(array):
        array = array.astype(bf16)
        return [array[r * rows : (r + 1) * rows] for r in range(count)]

    def token_sum(left, right):
        return jnp.einsum("tf,td->fd", left, right, preferred_element_type=f32).astype(bf16)

    def to_owners(part):
        return lax.psum_scatter(part, "shard", scatter_dimension=0, tiled=True)

    parts = split(jnp.dot(attended_rows, w_o, preferred_element_type=f32))
    kept, arrived = scatter_pieces(scatter_turn(scatter_start(parts)))
    middle, upper, lower = norm(kept, arrived, mine, gains[1:2])
    normed_mlp = jnp.concatenate(gather_halves(upper, lower), axis=0)
    normed_mlp, cot = tie(normed_mlp, cotangent[0])
    cot_near = gather_near(cot)
    gate_up = jnp.dot(normed_mlp, w_gu, preferred_element_type=f32)
    gate_up, cot_near = tie(gate_up, cot_near)
    cot_blocks, cot_far = gather_far(cot, cot_near)
    back_mlp = jnp.concatenate([*cot_blocks, *cot_far], axis=0)
    gate_lin, upward = gate_up[:, :width_f], gate_up[:, width_f:]
    sigmoid_gate = jax.nn.sigmoid(gate_lin)
    silu_gate = gate_lin * sigmoid_gate
    hidden = (silu_gate * upward).astype(bf16)
    down_part = token_sum(hidden, back_mlp)

    w_dn, down_part = tie(w_dn, down_part)
    own_down = to_owners(down_part)
    out_parts = split(jnp.dot(hidden, w_dn, preferred_element_type=f32))
    w_dn, out_parts = tie(w_dn, out_parts)
    kept, turning, straight = scatter_start(out_parts)
    back_hidden = (
        jnp.einsum("td,fd->tf", back_mlp, w_dn, preferred_element_type=f32).astype(bf16).astype(f32)
    )
    back_gate = back_hidden * upward * sigmoid_gate * (1.0 + gate_lin * (1.0 - sigmoid_gate))
    back_up = back_hidden * silu_gate
    back_gu = jnp.concatenate([back_gate.astype(bf16), back_up.astype(bf16)], axis=1)

    turning, back_gu = tie(turning, back_gu)
    kept, sent, straight = scatter_turn((kept, turning, straight))

    parts = split(jnp.einsum("tf,df->td", back_gu, w_gu, preferred_element_type=f32))
    parts, (sent, straight) = tie(parts, (sent, straight))
    output = (middle + scatter_end((kept, sent, straight))).astype(bf16)[None]
    parts, turning, straight = scatter_start(parts)
    gu_part = token_sum(normed_mlp, back_gu)
    (turning, straight), gu_part = tie((turning, straight), gu_part)
    state = scatter_turn((parts, turning, straight))
    own_gu = to_owners(gu_part)
    kept, arrived = scatter_pieces(state)

    back_middle, upper, lower = norm_back(kept, arrived, middle, cot, gains[1:2], True)
    pieces, own_down = tie(gather_halves(upper, lower), own_down)
    back_attended, *out_blocks = branch(place_arg, pieces, w_o, attended_t)
    out_blocks = [hop(one, r) if r else one for r, one in enumerate(out_blocks)]
    down_near = gather_near(own_down)
    back_query, back_kv = attend_back(
        place_arg, queries, keys, values, attended, back_attended, logsum, cosine, sine
    )
    back_query, (out_blocks, down_near) = tie(back_query, (out_blocks, down_near))
    back_query, back_kv = back_query.reshape(length, -1), back_kv.reshape(length, -1)
    parts = input_grads(back_query, back_kv, w_attn)
    down_blocks, down_far = gather_far(own_down, down_near)
    if count == 4:
        turning = (hop(parts[3], 1), hop(parts[4], 2))
        parts, back_query = tie(parts, back_query)
    attn_part = attention_grads(
        place_arg, normed.reshape(length, width), back_query, back_kv, out_blocks
    )
    if count == 4:
        (turning, down_far), attn_part = tie((turning, down_far), attn_part)
    attn_part, own_gu = tie(attn_part, own_gu)
    own_attn = to_owners(attn_part)
    gu_near = gather_near(own_gu)
    if count == 4:
        to_near = turn(parts[1:3], turning)
        to_near, gu_near = tie(to_near, gu_near)
        kept, arrived = parts[0], (hop(to_near[0], 1), hop(to_near[1], 2))
    else:
        kept, arrived = scatter_pieces(scatter_turn(scatter_start(parts)))
    gu_blocks, gu_far = gather_far(own_gu, gu_near)
    arrived, own_attn = tie(arrived, own_attn)
    (grad_tokens,) = norm_back(kept, arrived, mine, back_middle, gain_first, False)
    attn_late, grad_tokens = tie(own_attn, grad_tokens)
    attn_blocks = [own_attn] + [
        hop(own_attn if r in (1, 2) else attn_late, r) for r in range(1, count)
    ]

    grad_down = jnp.zeros((count * piece, width), f32)
    places = [((place ^ r) * piece, block) for r, block in enumerate(down_blocks)]
    for at, block in enumerate(down_far):
        places.append(((place ^ (count - 1)) * piece + at * (piece // 2), block))
    for at, block in places:
        grad_down = lax.dynamic_update_slice_in_dim(grad_down, block.astype(f32), at, axis=0)
    grad_gate, grad_up, grad_gain_mlp = put_columns(
        place_arg,
        gu_blocks,
        gu_far,
        w_gate,
        w_up,
        gain_mlp.reshape(1, -1),
        shards,
    )
    attn_blocks, (grad_gate, grad_up) = tie(attn_blocks, (grad_gate, grad_up))
    grad_query, grad_key, grad_value, grad_out, grad_gain_attn = put_attention(
        place_arg,
        attn_blocks,
        (),
        w_query,
        w_key,
        w_value,
        gain_attn.reshape(1, -1),
        width,
        copies,
    )
    return (
        output,
        grad_tokens[None],
        grad_query,
        grad_key,
        grad_value,
        grad_out,
        grad_gate,
        grad_up,
        grad_down,
        grad_gain_attn.reshape(-1),
        grad_gain_mlp.reshape(-1),
    )


def solution(mesh):
    rows = P("shard", "seq", None)
    weight = P("shard", None)
    gain = P("shard")
    in_specs = (rows,) + (weight,) * 7 + (gain, gain, rows)
    out_specs = (rows, rows) + (weight,) * 7 + (gain, gain)
    return jax.shard_map(
        on_device, mesh=mesh, in_specs=in_specs, out_specs=out_specs, check_vma=False
    )
```
